32 devices in a mesh: pair: 2 (over core), shot: 16 (over z, y, x).
Axes of the slice: x: 2, y: 2, z: 4, core: 2. Of those that a mesh axis runs over, the one named last changes fastest.
Arguments:
- records: bfloat16 [4, 384, 384, 128], P('pair', 'shot'), may hold values from -6 to 6
- surface: float32 [16, 384], P('shot'), may hold values from 0.4 to 1.2
- mirror: int32 [4], replicated, may hold values from 0 to 3, as said below
Outputs:
- predicted: bfloat16 [4, 384, 384, 128], P('pair', 'shot')
The draws below stay inside these ranges and needn't reach their ends.
Inputs may be any that keep to these rules, and one draw needn't show every extreme that they name: mirror is an involution without fixed points: mirror[mirror[g]] = g and mirror[g] differs from g for every group.
All inputs are finite; a program needn't handle non-finite values.
Results may differ from the reference program's by a relative error of at most 0.0088.
Values may be sent and summed in bfloat16 or wider, within the bound.
A program may use at most 128 MiB of HBM per device.

```python
import math
import jax
import jax.numpy as jnp
from jax import lax

SHOTS = 384
RECV = 384
TIME = 128
FREQS = 16
ORDERS = 2
GROUPS = 4


def draw_mirror(key, part):
    order = jax.random.permutation(key, GROUPS).astype(jnp.int32)
    evens = order[0::2]
    odds = order[1::2]
    paired = jnp.zeros((GROUPS,), jnp.int32).at[evens].set(odds).at[odds].set(evens)
    return paired


def block_scale(key, extent, split, low, high):
    def one(dim, parts):
        heights = jax.random.uniform(jax.random.fold_in(jax.random.fold_in(key, 6), dim), (parts,), jnp.float32, low / len(split), high / len(split))
        return jnp.repeat(jnp.exp(heights), extent[dim] // parts).reshape((-1,) + (1,) * (len(extent) - dim - 1))

    gain = one(*split[0])
    for cut in split[1:]:
        gain = gain * one(*cut)
    return gain


def noise(stream_key, shape, width, reach, cuts=(), held_as=jnp.bfloat16):
    entries = jax.random.normal(stream_key, shape, jnp.float32) * width
    if len(cuts) > 0:
        entries = block_scale(stream_key, shape, cuts, -0.22, 0.18) * entries
    return jnp.clip(entries, min=-reach, max=reach).astype(held_as)


def setup_inputs(seed: int = 0) -> dict:
    streams_of = jax.random.split(jax.random.key(seed), 4)
    records = noise(streams_of[0], (GROUPS, SHOTS, RECV, TIME), 1.0, 6.0, ((0, 2), (1, 16)))
    surface = jnp.clip(jnp.exp(math.log(1.2) - 1.0986123 * jax.random.uniform(streams_of[1], (FREQS, RECV), jnp.float32) ** block_scale(streams_of[1], (FREQS, RECV), ((0, 16),), -0.2, 0.2)), 0.4, 1.2)
    mirror = draw_mirror(jax.random.fold_in(streams_of[3], 71), 0)
    return dict(records=records, surface=surface, mirror=mirror)


def make_tables(freqs, time):
    product = jnp.arange(1, freqs + 1, dtype=jnp.int32)[:, None] * jnp.arange(time, dtype=jnp.int32)[None, :] % time
    phase = product.astype(jnp.float32) * (2.0 * math.pi / time)
    cosine = jnp.cos(phase)
    sine = jnp.sin(phase)
    forward = (jnp.stack([cosine, -sine], axis=1) * math.sqrt(2.0 / time)).astype(jnp.bfloat16)
    inverse = (jnp.stack([cosine, -sine], axis=1) / math.sqrt(freqs)).astype(jnp.bfloat16)
    return (forward, inverse)

def real_dot(left, right):
    return jnp.dot(left.astype(jnp.float32), right.astype(jnp.float32), precision=lax.Precision.HIGHEST)

def one_frequency(items):
    own_spec, mate_spec, column_scale = items
    left = (own_spec.astype(jnp.float32) * column_scale[None, None, :]).astype(jnp.bfloat16)
    total = jnp.zeros(own_spec.shape, jnp.float32)
    for order_index in range(ORDERS):
        real_part = real_dot(left[0], mate_spec[0]) - real_dot(left[1], mate_spec[1])
        imag_part = real_dot(left[0], mate_spec[1]) + real_dot(left[1], mate_spec[0])
        product = jnp.stack([real_part, imag_part], axis=0)
        total = total + product
        if order_index + 1 < ORDERS:
            left = (product * column_scale[None, None, :]).astype(jnp.bfloat16)
    return total.astype(jnp.bfloat16)

def reference(records, surface, mirror):
    forward, inverse = make_tables(FREQS, TIME)

    def group_spectra(group_records):
        return jnp.einsum('kct,srt->kcsr', forward.astype(jnp.float32), group_records.astype(jnp.float32), precision=lax.Precision.HIGHEST).astype(jnp.bfloat16)
    spectra = lax.map(group_spectra, records)
    mates = spectra[mirror]
    scale = -surface.astype(jnp.float32) / math.sqrt(2.0 * RECV)

    def one_group(items):
        own_group, mate_group = items
        totals = lax.map(one_frequency, (own_group, mate_group, scale))
        predicted = jnp.einsum('kcsr,kct->srt', totals.astype(jnp.float32), inverse.astype(jnp.float32), precision=lax.Precision.HIGHEST)
        return predicted.astype(jnp.bfloat16)
    return lax.map(one_group, (spectra, mates))
```

```python
import functools
import math

import jax
import jax.numpy as jnp
from jax import lax
from jax.experimental import pallas as pl
from jax.experimental.pallas import tpu as pltpu
from jax.sharding import PartitionSpec as P

ORDERS = 2
MESH = pl.DeviceIdType.MESH
VMEM_BYTES = 67043328
LANES = 128


def make_tables(freqs, time):
    row = lax.broadcasted_iota(jnp.int32, (2 * freqs, time), 0)
    product = (row // 2 + 1) * lax.broadcasted_iota(jnp.int32, (2 * freqs, time), 1) % time
    phase = product.astype(jnp.float32) * (2.0 * math.pi / time)
    wave = jnp.where(row % 2 == 0, jnp.cos(phase), -jnp.sin(phase))
    forward = (wave * math.sqrt(2.0 / time)).astype(jnp.bfloat16)
    inverse = (wave / math.sqrt(freqs)).astype(jnp.bfloat16)
    return (forward, inverse)


def kernel(chips, cores, lanes, stages, mirror_hbm, surface_hbm, forward_ref, inverse_ref, records_ref, out_ref, *scratch):
    held = scratch[:lanes]
    stage = scratch[lanes : lanes + stages]
    (
        send, left, block, first, totals, back, surface_ref, mirror_ref,
        small_sems, load_sems, own_sems, send_sems, recv_sems, lane_sems, lane_recv_sems,
        pass_sems, pass_recv_sems, back_own_sems, back_send_sems, back_recv_sems, surface_sems,
    ) = scratch[lanes + stages :]
    me = lax.axis_index("shot")
    core = lax.axis_index("pair")
    _, groups, parts, shots, width = send.shape
    freqs = parts // 2
    columns = chips // lanes
    half = columns // 2
    rows = chips * parts
    strips = width // LANES
    loads = load_sems.shape[1]
    chunk = shots // loads
    lane = lax.rem(me, lanes)
    column = me // lanes
    side = column // half

    def lanes_of(strip):
        return slice(strip * LANES, (strip + 1) * LANES)

    def chip(there):
        return there * lanes + lane

    def beside(step):
        return column * lanes + lax.rem(lane + step, lanes)

    def peer(step):
        return lax.rem(core + step, cores)

    def away(index):
        return (1 - side) * half + lax.rem(index + column, half)

    def away_in_order(index):
        return (1 - side) * half + index

    def near(index):
        return side * half + lax.rem(index + column, half)

    def load(group, index):
        some = pl.ds(index * chunk, chunk)
        return pltpu.make_async_copy(
            records_ref.at[group, some], out_ref.at[group, some], load_sems.at[group, index]
        )

    for group in range(groups):
        for index in range(loads):
            load(group, index).start()
    surface_copy = pltpu.make_async_copy(surface_hbm, surface_ref.at[lane], small_sems.at[0])
    mirror_copy = pltpu.make_async_copy(mirror_hbm, mirror_ref, small_sems.at[1])
    surface_copy.start()
    mirror_copy.start()

    barrier = pltpu.get_barrier_semaphore()

    @pl.loop(1, columns)
    def _(step):
        there = lax.rem(column + step, columns)
        pl.semaphore_signal(barrier, inc=1, device_id=(core, chip(there)), device_id_type=MESH)

    for step in range(1, lanes):
        pl.semaphore_signal(barrier, inc=1, device_id=(core, beside(step)), device_id_type=MESH)
    for step in range(1, cores):
        pl.semaphore_signal(barrier, inc=1, device_id=(peer(step), me), device_id_type=MESH)

    def spread(phase, group, source, target):
        return pltpu.make_async_remote_copy(
            src_ref=send.at[target * lanes + phase, group],
            dst_ref=held[phase].at[core, group, :, source, lane],
            send_sem=send_sems.at[phase, group, target],
            recv_sem=recv_sems.at[phase, group, source],
            device_id=(core, chip(target)),
            device_id_type=MESH,
        )

    def keep(phase, group):
        return pltpu.make_async_copy(
            send.at[column * lanes + phase, group],
            held[phase].at[core, group, :, column, lane],
            own_sems.at[phase, group],
        )

    def lane_on(phase, group, source, source_lane, step):
        return pltpu.make_async_remote_copy(
            src_ref=held[phase].at[core, group, :, source, source_lane],
            dst_ref=held[phase].at[core, group, :, source, source_lane],
            send_sem=lane_sems.at[phase, group, step, source],
            recv_sem=lane_recv_sems.at[phase, group, step, source],
            device_id=(core, beside(step)),
            device_id_type=MESH,
        )

    def hand_on(phase, group, source, source_lane, other):
        return pltpu.make_async_remote_copy(
            src_ref=held[phase].at[core, group, :, source, source_lane],
            dst_ref=held[phase].at[core, group, :, source, source_lane],
            send_sem=pass_sems.at[phase, group, other - 1, source, source_lane],
            recv_sem=pass_recv_sems.at[phase, group, other - 1, source, source_lane],
            device_id=(peer(other), me),
            device_id_type=MESH,
        )

    def pass_on(phase, group, source, source_lane):
        for other in range(1, cores):
            hand_on(phase, group, source, source_lane, other).start()

    def send_back(phase, group, source, target):
        return pltpu.make_async_remote_copy(
            src_ref=totals.at[phase, target, group],
            dst_ref=back.at[source * lanes + phase, group],
            send_sem=back_send_sems.at[phase, group, target],
            recv_sem=back_recv_sems.at[phase, group, source],
            device_id=(core, chip(target)),
            device_id_type=MESH,
        )

    def keep_back(phase, group):
        return pltpu.make_async_copy(
            totals.at[phase, column, group],
            back.at[column * lanes + phase, group],
            back_own_sems.at[phase, group],
        )

    def to_all(start, away=away):
        @pl.loop(0, half)
        def _(index):
            start(away(index))

        @pl.loop(1, half)
        def _(index):
            start(near(index))

    def spectra(group):
        for index in range(loads):
            load(group, index).wait()
            for shot in range(index * chunk, (index + 1) * chunk):
                value = lax.dot_general(
                    forward_ref[...], out_ref[group, shot], (((1,), (1,)), ((), ())),
                    preferred_element_type=jnp.float32,
                )
                for strip in range(strips):
                    stage[0][strip, shot * rows : (shot + 1) * rows] = value[:, lanes_of(strip)]
        for row in range(rows):
            for strip in range(strips):
                send[row // parts, group, row % parts, :, lanes_of(strip)] = (
                    stage[0][strip, pl.ds(row, shots, stride=rows), :].astype(jnp.bfloat16)
                )

    def spread_all(phase, group):
        to_all(lambda target: spread(phase, group, column, target).start())
        keep(phase, group).start()

    def relay(phase, group):
        def step_on(source):
            for step in range(1, lanes):
                lane_on(phase, group, source, lane, step).start()
            pass_on(phase, group, source, lane)

        keep(phase, group).wait()
        step_on(column)

        @pl.loop(1, half)
        def _(index):
            source = near(index)
            spread(phase, group, source, source).wait_recv()
            step_on(source)

        @pl.loop(0, half)
        def _(index):
            source = away(index)
            spread(phase, group, source, source).wait_recv()
            step_on(source)

        if lanes > 1:
            @pl.loop(0, columns)
            def _(index):
                source = lax.rem(column + index, columns)
                for step in range(1, lanes):
                    source_lane = lax.rem(lane + lanes - step, lanes)
                    lane_on(phase, group, source, source_lane, step).wait_recv()
                    pass_on(phase, group, source, source_lane)

    def settle(phase):
        @pl.loop(0, columns)
        def _(source):
            for group in range(groups):
                for source_lane in range(lanes):
                    for other in range(1, cores):
                        hand_on(phase, group, source, source_lane, other).wait_recv()

    def matrix(value):
        value = value.astype(jnp.float32)
        return value.reshape(-1, width)

    tall = chips * shots
    tile = width if width % 256 == 0 else 2 * width

    def predict(phase, group):
        mate = mirror_ref[core * groups + group]
        mate_slot = mate // groups
        mate_group = lax.rem(mate, groups)
        for freq in range(freqs):
            scale = -surface_ref[phase, pl.ds(freq, 1), :] / math.sqrt(2.0 * width)
            mate_re = matrix(held[phase][mate_slot, mate_group, 2 * freq])
            mate_im = matrix(held[phase][mate_slot, mate_group, 2 * freq + 1])
            block[:tall, :width] = mate_re.astype(jnp.bfloat16)
            block[tall:, width:] = mate_re.astype(jnp.bfloat16)
            block[:tall, width:] = mate_im.astype(jnp.bfloat16)
            block[tall:, :width] = (-mate_im).astype(jnp.bfloat16)
            for part in range(2):
                value = matrix(held[phase][core, group, 2 * freq + part, :, lane])
                left[:, part * width : (part + 1) * width] = (value * scale).astype(jnp.bfloat16)
            span = 16 if columns % 16 == 0 else columns
            for order in range(ORDERS):
                for top in range(0, columns, span):
                    band = slice(top * shots, (top + span) * shots)
                    pieces = []
                    for start in range(0, 2 * width, tile):
                        piece = jnp.dot(
                            left[band, :], block[:, start : start + tile],
                            preferred_element_type=jnp.float32,
                        )
                        if order > 0:
                            piece = piece + first[band, start : start + tile]
                        if order + 1 < ORDERS:
                            first[band, start : start + tile] = piece
                            pieces.append(piece)
                        else:
                            for low in range(start, start + tile, width):
                                total = piece[:, low - start : low - start + width]
                                totals[phase, top : top + span, group, 2 * freq + low // width] = (
                                    total.reshape(span, shots, width).astype(jnp.bfloat16)
                                )
                    if order + 1 < ORDERS:
                        product = jnp.concatenate(pieces, axis=1) if len(pieces) > 1 else pieces[0]
                        wide = jnp.concatenate([scale, scale], axis=1)
                        left[band, :] = (product * wide).astype(jnp.bfloat16)
        last = phase + 1 == lanes and group + 1 == groups
        to_all(
            lambda target: send_back(phase, group, column, target).start(),
            away_in_order if last else away,
        )
        keep_back(phase, group).start()

    def collect(phase, group):
        here = stage[group % stages]

        def unpack(source):
            place = source * lanes + phase
            for part in range(parts):
                value = back[place, group, part].astype(jnp.float32)
                for strip in range(strips):
                    here[strip, pl.ds(place * parts + part, shots, stride=rows), :] = (
                        value[:, lanes_of(strip)]
                    )

        keep_back(phase, group).wait()
        unpack(column)

        @pl.loop(1, half)
        def _(index):
            source = near(index)
            send_back(phase, group, source, source).wait_recv()
            unpack(source)

        @pl.loop(0, half)
        def _(index):
            source = away(index)
            send_back(phase, group, source, source).wait_recv()
            unpack(source)

    def invert(group):
        here = stage[group % stages]
        for shot in range(shots):
            for strip in range(strips):
                value = here[strip, shot * rows : (shot + 1) * rows].astype(jnp.bfloat16)
                out_ref[group, shot, lanes_of(strip), :] = lax.dot_general(
                    value, inverse_ref[...], (((0,), (0,)), ((), ())),
                    preferred_element_type=jnp.float32,
                ).astype(jnp.bfloat16)

    def surface_on(step, source_lane):
        return pltpu.make_async_remote_copy(
            src_ref=surface_ref.at[source_lane],
            dst_ref=surface_ref.at[source_lane],
            send_sem=surface_sems.at[0, step],
            recv_sem=surface_sems.at[1, step],
            device_id=(core, beside(step)),
            device_id_type=MESH,
        )

    for group in range(groups):
        spectra(group)
        if group == 0:
            pl.semaphore_wait(barrier, columns + lanes + cores - 3)
        spread_all(0, group)
    for phase in range(1, lanes):
        for group in range(groups):
            spread_all(phase, group)

    surface_copy.wait()
    mirror_copy.wait()
    for step in range(1, lanes):
        surface_on(step, lane).start()
    for group in range(groups):
        relay(0, group)
    for step in range(1, lanes):
        surface_on(step, lax.rem(lane + lanes - step, lanes)).wait_recv()
    settle(0)
    for phase in range(lanes):
        for group in range(groups):
            predict(phase, group)
            if phase + 1 < lanes:
                relay(phase + 1, group)
        if phase + 1 < lanes:
            settle(phase + 1)

    for step in range(1, lanes):
        surface_on(step, lane).wait_send()

    @pl.loop(0, columns)
    def _(source):
        for phase in range(lanes):
            for group in range(groups):
                for step in range(1, lanes):
                    lane_on(phase, group, source, lane, step).wait_send()
                for source_lane in range(lanes):
                    for other in range(1, cores):
                        hand_on(phase, group, source, source_lane, other).wait_send()

                @pl.when(source != column)
                def _():
                    spread(phase, group, column, source).wait_send()

    for phase in range(lanes - 1):
        for group in range(groups):
            collect(phase, group)
    for group in range(groups):
        collect(lanes - 1, group)
        invert(group)

    @pl.loop(0, columns)
    def _(target):
        @pl.when(target != column)
        def _():
            for phase in range(lanes):
                for group in range(groups):
                    send_back(phase, group, column, target).wait_send()


def local(records, surface, mirror):
    chips = lax.axis_size("shot")
    cores = lax.axis_size("pair")
    groups, shots, receivers, time = records.shape
    freqs = surface.shape[0]
    parts = 2 * freqs
    forward, inverse = make_tables(freqs * chips, time)
    loads = 4 if shots % 4 == 0 else 1
    dma = pltpu.SemaphoreType.DMA

    def buffers(lanes, stages):
        columns = chips // lanes
        tall = columns * shots
        held = ((cores, groups, parts, columns, lanes, shots, receivers), jnp.bfloat16)
        stage = ((receivers // LANES, shots * chips * parts, LANES), jnp.float32)
        return [held] * lanes + [stage] * stages + [
            ((chips, groups, parts, shots, receivers), jnp.bfloat16),
            ((tall, 2 * receivers), jnp.bfloat16),
            ((2 * chips * shots, 2 * receivers), jnp.bfloat16),
            ((tall, 2 * receivers), jnp.float32),
            ((lanes, columns, groups, parts, shots, receivers), jnp.bfloat16),
            ((chips, groups, parts, shots, receivers), jnp.bfloat16),
            ((lanes, freqs, receivers), jnp.float32),
        ]

    def size(shapes):
        return sum(math.prod(shape) * jnp.dtype(kind).itemsize for shape, kind in shapes)

    lanes, stages = 2, groups
    scratch = buffers(lanes, stages)
    out_bytes = records.size * records.dtype.itemsize
    roomy = chips % 4 == 0 and out_bytes + size(scratch) < 40 * 1024 * 1024
    if not roomy:
        lanes, stages = 1, 1
        scratch = buffers(lanes, stages)
    columns = chips // lanes
    grant = min(size(scratch) + 8 * 1024 * 1024, VMEM_BYTES) if roomy else VMEM_BYTES
    out_shape = pltpu.VMEM if roomy else jax.ShapeDtypeStruct
    each = (lanes, groups)
    return pl.pallas_call(
        functools.partial(kernel, chips, cores, lanes, stages),
        out_shape=out_shape(records.shape, jnp.bfloat16),
        in_specs=[
            pl.BlockSpec(memory_space=pltpu.HBM),
            pl.BlockSpec(memory_space=pltpu.HBM),
            pl.BlockSpec(memory_space=pltpu.VMEM),
            pl.BlockSpec(memory_space=pltpu.VMEM),
            pl.BlockSpec(memory_space=pltpu.HBM),
        ],
        out_specs=pl.BlockSpec(memory_space=pltpu.VMEM),
        scratch_shapes=[
            *(pltpu.VMEM(shape, kind) for shape, kind in scratch),
            pltpu.SMEM(mirror.shape, jnp.int32),
            dma((2,)),
            dma((groups, loads)),
            dma(each),
            dma((*each, columns)),
            dma((*each, columns)),
            dma((*each, lanes, columns)),
            dma((*each, lanes, columns)),
            dma((*each, cores - 1, columns, lanes)),
            dma((*each, cores - 1, columns, lanes)),
            dma(each),
            dma((*each, columns)),
            dma((*each, columns)),
            dma((2, lanes)),
        ],
        compiler_params=pltpu.CompilerParams(
            collective_id=0, has_side_effects=True, vmem_limit_bytes=grant
        ),
    )(
        pltpu.with_memory_space_constraint(mirror, pltpu.HBM),
        pltpu.with_memory_space_constraint(surface, pltpu.HBM),
        forward,
        inverse,
        pltpu.with_memory_space_constraint(records, pltpu.HBM),
    )


def solution(mesh):
    return jax.shard_map(
        local,
        mesh=mesh,
        in_specs=(P("pair", "shot", None, None), P("shot", None), P()),
        out_specs=P("pair", "shot", None, None),
        check_vma=False,
    )
```

```python
import functools
import math

import jax
import jax.numpy as jnp
import numpy as np
from jax import lax
from jax.experimental import pallas as pl
from jax.experimental.pallas import tpu as pltpu
from jax.sharding import PartitionSpec as P

ORDERS = 2
MESH = pl.DeviceIdType.MESH
VMEM_BYTES = 67043328
LANES = 128


def make_tables(freqs, time):
    row = np.arange(2 * freqs)[:, None]
    product = (row // 2 + 1) * np.arange(time)[None, :] % time
    phase = product.astype(np.float32) * np.float32(2.0 * math.pi / time)
    wave = np.where(row % 2 == 0, np.cos(phase), -np.sin(phase))
    forward = (wave * math.sqrt(2.0 / time)).astype(jnp.bfloat16)
    inverse = (wave / math.sqrt(freqs)).astype(jnp.bfloat16)
    return np.stack([forward, inverse])


def cut(shots, group, groups):
    whole = ((0, shots),)
    if shots % 8 or shots < 16:
        return whole, whole
    first = ((0, 8), (8, shots - 8)) if group == 0 else whole
    last = ((0, shots - 8), (shots - 8, 8)) if group + 1 == groups else whole
    return first, last


def kernel(
    chips, cores, mirror_hbm, surface_hbm, tables_hbm, records_ref, out_ref,
    traces, stage, send, held, left, block, first, totals, back, surface_ref, tables, mirror_ref,
    small_sems, load_sems, own_sems, send_sem, recv_sems, pass_sems, back_send_sem, back_recv_sems, out_sem,
    entered,
):
    me = lax.axis_index("shot")
    core = lax.axis_index("pair")
    groups, parts, shots, width = send.shape[1:]
    freqs = parts // 2
    rows = chips * parts
    strips = width // LANES
    half = chips // 2
    quarter = chips // 4
    across = jnp.where(me < half, 0, 1)
    plane = me // quarter
    planes = (plane, plane + 1 - 2 * lax.rem(plane, 2), 3 * (1 - across), 2 - across)
    cuts = [cut(shots, group, groups) for group in range(groups)]

    def strip_of(strip):
        return slice(strip * LANES, (strip + 1) * LANES)

    def level(step):
        return plane * quarter + lax.rem(me + step, quarter)

    def upright(there):
        return there * quarter + lax.rem(me, quarter)

    def peer(step):
        return lax.rem(core + step, cores)

    def turned(index, size):
        inner = lax.rem(index + me, size) + size * (index // size)
        return lax.rem(across * size + inner, 2 * size)

    def middle(index):
        return quarter + turned(index, quarter)

    def outer(index):
        place = turned(index, quarter)
        return jnp.where(place < quarter, place, place + half)

    def load(group, index):
        some = pl.ds(*cuts[group][0][index])
        return pltpu.make_async_copy(
            records_ref.at[group, some], traces.at[group, some], load_sems.at[group, index]
        )

    for group in range(groups):
        for index in range(len(cuts[group][0])):
            load(group, index).start()
    surface_copy = pltpu.make_async_copy(surface_hbm, surface_ref, small_sems.at[0])
    mirror_copy = pltpu.make_async_copy(mirror_hbm, mirror_ref, small_sems.at[1])
    tables_copy = pltpu.make_async_copy(tables_hbm, tables, small_sems.at[2])
    tables_copy.start()
    surface_copy.start()
    mirror_copy.start()

    barrier = pltpu.get_barrier_semaphore()

    @pl.loop(1, quarter)
    def _(step):
        pl.semaphore_signal(barrier, inc=1, device_id=(core, level(step)), device_id_type=MESH)

    for step in range(1, 4):
        pl.semaphore_signal(barrier, inc=1, device_id=(core, upright(planes[step])), device_id_type=MESH)
    for step in range(1, cores):
        pl.semaphore_signal(barrier, inc=1, device_id=(peer(step), me), device_id_type=MESH)

    def spread(source, target, group, some):
        return pltpu.make_async_remote_copy(
            src_ref=send.at[target, group, :, some],
            dst_ref=held.at[core, group, :, source, some],
            send_sem=send_sem,
            recv_sem=recv_sems.at[group, source // quarter],
            device_id=(core, target),
            device_id_type=MESH,
        )

    def arrived(group, there, count):
        some = held.at[core, group, :, pl.ds(0, count)]
        return pltpu.make_async_remote_copy(
            src_ref=some,
            dst_ref=some,
            send_sem=send_sem,
            recv_sem=recv_sems.at[group, there],
            device_id=(core, me),
            device_id_type=MESH,
        )

    def hand_on(some, other):
        return pltpu.make_async_remote_copy(
            src_ref=some,
            dst_ref=some,
            send_sem=pass_sems.at[other - 1, 0],
            recv_sem=pass_sems.at[other - 1, 1],
            device_id=(peer(other), me),
            device_id_type=MESH,
        )

    def keep(group):
        return pltpu.make_async_copy(
            send.at[me, group], held.at[core, group, :, me], own_sems.at[group]
        )

    def send_back(source, target, group, index):
        some = pl.ds(*cuts[group][1][index])
        return pltpu.make_async_remote_copy(
            src_ref=totals.at[target, group, :, some],
            dst_ref=back.at[source, group, :, some],
            send_sem=back_send_sem,
            recv_sem=back_recv_sems.at[group, index, source // quarter],
            device_id=(core, target),
            device_id_type=MESH,
        )

    def returned(group, index, there, count):
        some = back.at[pl.ds(0, count), group, :, pl.ds(*cuts[group][1][index])]
        return pltpu.make_async_remote_copy(
            src_ref=some,
            dst_ref=some,
            send_sem=back_send_sem,
            recv_sem=back_recv_sems.at[group, index, there],
            device_id=(core, me),
            device_id_type=MESH,
        )

    def sent(buffer, sem):
        some = buffer.at[pl.ds(0, chips - 1)]
        return pltpu.make_async_remote_copy(
            src_ref=some,
            dst_ref=some,
            send_sem=sem,
            recv_sem=recv_sems.at[0, 0],
            device_id=(core, me),
            device_id_type=MESH,
        )

    def give(group, index):
        some = pl.ds(*cuts[group][1][index])
        return pltpu.make_async_copy(
            traces.at[group, some], out_ref.at[group, some], out_sem
        )

    def spread_half(target_of, group):
        @pl.loop(0, half)
        def _(step):
            target = target_of(step)

            @pl.when(lax.rem(target, quarter) != lax.rem(me, quarter) if group == 0 else target != me)
            def _():
                spread(me, target, group, pl.ds(0, shots)).start()

    def spectra(group, index):
        start, size = cuts[group][0][index]
        load(group, index).wait()
        for shot in range(start, start + size):
            value = lax.dot_general(
                tables[0], traces[group, shot], (((1,), (1,)), ((), ())),
                preferred_element_type=jnp.float32,
            )
            for strip in range(strips):
                stage[strip, shot * rows : (shot + 1) * rows] = value[:, strip_of(strip)]
        for row in range(rows):
            for strip in range(strips):
                value = stage[strip, pl.ds(start * rows + row, size, stride=rows), :]
                send[row // parts, group, row % parts, start : start + size, strip_of(strip)] = (
                    value.astype(jnp.bfloat16)
                )

    tables_copy.wait()
    for index in range(len(cuts[0][0])):
        spectra(0, index)
        if index == 0:
            pl.semaphore_wait(barrier, quarter + 2 + cores - 1)

            @pl.loop(1, quarter)
            def _(step):
                pl.semaphore_signal(entered, inc=1, device_id=(core, level(step)), device_id_type=MESH)

        for order in (3, 2, 1):
            spread(me, upright(planes[order]), 0, pl.ds(*cuts[0][0][index])).start()
    keep(0).start()
    pl.semaphore_wait(entered, quarter - 1)
    spread_half(middle, 0)
    for group in range(1, groups):
        for index in range(len(cuts[group][0])):
            spectra(group, index)
        spread_half(middle, group)
        keep(group).start()
    for group in range(groups):
        spread_half(outer, group)

    surface_copy.wait()
    mirror_copy.wait()
    for group in range(groups):
        for order, there in enumerate(planes):
            if order == 0:
                keep(group).wait()
            arrived(group, there, quarter - 1 if order == 0 else quarter).wait_recv()
            for other in range(1, cores):
                hand_on(held.at[core, group, :, pl.ds(there * quarter, quarter)], other).start()
    for other in range(1, cores):
        hand_on(held.at[core], other).wait()

    def matrix(slot, group, part):
        value = held[slot, group, part].astype(jnp.float32)
        return value.reshape(chips * shots, width)

    tall = chips * shots
    span = 16 if chips % 16 == 0 else chips
    tile = width if width % 256 == 0 else 2 * width
    for group in range(groups):
        mate = mirror_ref[core * groups + group]
        mate_slot = mate // groups
        mate_group = lax.rem(mate, groups)
        for freq in range(freqs):
            scale = -surface_ref[pl.ds(freq, 1), :] / math.sqrt(2.0 * width)
            mate_re = matrix(mate_slot, mate_group, 2 * freq)
            mate_im = matrix(mate_slot, mate_group, 2 * freq + 1)
            block[:tall, :width] = mate_re.astype(jnp.bfloat16)
            block[tall:, width:] = mate_re.astype(jnp.bfloat16)
            block[:tall, width:] = mate_im.astype(jnp.bfloat16)
            block[tall:, :width] = (-mate_im).astype(jnp.bfloat16)
            for part in range(2):
                columns = slice(part * width, (part + 1) * width)
                value = matrix(core, group, 2 * freq + part)
                left[:, columns] = (value * scale).astype(jnp.bfloat16)
            for order in range(ORDERS):
                for top in range(0, chips, span):
                    band = slice(top * shots, (top + span) * shots)
                    pieces = []
                    for start in range(0, 2 * width, tile):
                        piece = jnp.dot(
                            left[band, :], block[:, start : start + tile],
                            preferred_element_type=jnp.float32,
                        )
                        if order > 0:
                            piece = piece + first[band, start : start + tile]
                        if order + 1 < ORDERS:
                            first[band, start : start + tile] = piece
                            pieces.append(piece)
                        else:
                            for low in range(start, start + tile, width):
                                total = piece[:, low - start : low - start + width]
                                totals[top : top + span, group, 2 * freq + low // width] = (
                                    total.reshape(span, shots, width).astype(jnp.bfloat16)
                                )
                    if order + 1 < ORDERS:
                        product = jnp.concatenate(pieces, axis=1) if len(pieces) > 1 else pieces[0]
                        wide = jnp.concatenate([scale, scale], axis=1)
                        left[band, :] = (product * wide).astype(jnp.bfloat16)

        last = group + 1 == groups
        pieces = range(len(cuts[group][1]))
        if last:
            for index in pieces:
                send_back(me, (1 - across) * half, group, index).start()
        for index in pieces:

            @pl.loop(1 if last else 0, chips)
            def _(step):
                target = lax.rem((1 - across) * half + step, chips) if last else turned(step, half)

                @pl.when(target != me)
                def _():
                    send_back(me, target, group, index).start()

    sent(send, send_sem).wait_send()

    for group in range(groups):
        for index, (start, size) in enumerate(cuts[group][1]):

            def unpack(buffer, source):
                for part in range(parts):
                    value = buffer[source, group, part, start : start + size].astype(jnp.float32)
                    place = start * rows + source * parts + part
                    for strip in range(strips):
                        stage[strip, pl.ds(place, size, stride=rows), :] = value[:, strip_of(strip)]

            unpack(totals, me)
            for order, there in enumerate(planes):
                returned(group, index, there, quarter - 1 if order == 0 else quarter).wait_recv()

                @pl.loop(1 if order == 0 else 0, quarter)
                def _(step):
                    unpack(back, there * quarter + lax.rem(me + step, quarter))

            for shot in range(start, start + size):
                for strip in range(strips):
                    value = stage[strip, shot * rows : (shot + 1) * rows].astype(jnp.bfloat16)
                    traces[group, shot, strip_of(strip), :] = lax.dot_general(
                        value, tables[1], (((0,), (0,)), ((), ())),
                        preferred_element_type=jnp.float32,
                    ).astype(jnp.bfloat16)
            give(group, index).start()

    sent(totals, back_send_sem).wait_send()
    pltpu.make_async_copy(traces, out_ref, out_sem).wait()


def local(records, surface, mirror):
    chips = lax.axis_size("shot")
    cores = lax.axis_size("pair")
    groups, shots, receivers, time = records.shape
    freqs = surface.shape[0]
    parts = 2 * freqs
    tables = jnp.asarray(make_tables(freqs * chips, time))
    tall = chips * shots
    block_shape = (chips, groups, parts, shots, receivers)
    dma = pltpu.SemaphoreType.DMA
    scratch = [
        (records.shape, jnp.bfloat16),
        ((receivers // LANES, shots * chips * parts, LANES), jnp.float32),
        (block_shape, jnp.bfloat16),
        ((cores, groups, parts, chips, shots, receivers), jnp.bfloat16),
        ((tall, 2 * receivers), jnp.bfloat16),
        ((2 * tall, 2 * receivers), jnp.bfloat16),
        ((tall, 2 * receivers), jnp.float32),
        (block_shape, jnp.bfloat16),
        (block_shape, jnp.bfloat16),
    ]
    held_bytes = sum(math.prod(shape) * jnp.dtype(kind).itemsize for shape, kind in scratch)
    roomy = held_bytes < 24 * 1024 * 1024
    grant = held_bytes + 8 * 1024 * 1024 if roomy else VMEM_BYTES
    out_shape = pltpu.VMEM if roomy else jax.ShapeDtypeStruct
    hbm = pl.BlockSpec(memory_space=pltpu.HBM)
    return pl.pallas_call(
        functools.partial(kernel, chips, cores),
        out_shape=out_shape(records.shape, jnp.bfloat16),
        in_specs=[hbm] * 4,
        out_specs=pl.BlockSpec(memory_space=pl.ANY),
        scratch_shapes=[
            *(pltpu.VMEM(shape, kind) for shape, kind in scratch),
            pltpu.VMEM(surface.shape, jnp.float32),
            pltpu.VMEM(tables.shape, tables.dtype),
            pltpu.SMEM(mirror.shape, jnp.int32),
            dma((3,)),
            dma((groups, 2)),
            dma((groups,)),
            dma,
            dma((groups, 4)),
            dma((max(cores - 1, 1), 2)),
            dma,
            dma((groups, 2, 4)),
            dma,
            pltpu.SemaphoreType.REGULAR,
        ],
        compiler_params=pltpu.CompilerParams(
            collective_id=0, has_side_effects=True, vmem_limit_bytes=grant
        ),
    )(
        pltpu.with_memory_space_constraint(mirror, pltpu.HBM),
        pltpu.with_memory_space_constraint(surface, pltpu.HBM),
        pltpu.with_memory_space_constraint(tables, pltpu.HBM),
        pltpu.with_memory_space_constraint(records, pltpu.HBM),
    )


def solution(mesh):
    return jax.shard_map(
        local,
        mesh=mesh,
        in_specs=(P("pair", "shot", None, None), P("shot", None), P()),
        out_specs=P("pair", "shot", None, None),
        check_vma=False,
    )
```

```python
import functools
import math

import jax
import jax.numpy as jnp
import numpy as np
from jax import lax
from jax.experimental import pallas as pl
from jax.experimental.pallas import tpu as pltpu
from jax.sharding import PartitionSpec as P

ORDERS = 2
MESH = pl.DeviceIdType.MESH
VMEM_BYTES = 67043328
LANES = 128


def make_tables(freqs, time):
    row = np.arange(2 * freqs)[:, None]
    product = (row // 2 + 1) * np.arange(time)[None, :] % time
    phase = product.astype(np.float32) * np.float32(2.0 * math.pi / time)
    wave = np.where(row % 2 == 0, np.cos(phase), -np.sin(phase))
    forward = (wave * math.sqrt(2.0 / time)).astype(jnp.bfloat16)
    inverse = (wave / math.sqrt(freqs)).astype(jnp.bfloat16)
    return np.stack([forward, inverse])


def cut(shots, group, groups):
    whole = ((0, shots),)
    if shots % 8 or shots < 16:
        return whole, whole
    first = tuple((start, 8) for start in range(0, shots, 8)) if group == 0 else whole
    last = ((0, shots - 8), (shots - 8, 8)) if group + 1 == groups else whole
    return first, last


def inverse(value, table):
    total = lax.dot_general(
        value.astype(jnp.bfloat16), table, (((0,), (0,)), ((), ())),
        preferred_element_type=jnp.float32,
    )
    return total.astype(jnp.bfloat16)


def finish(some_ref, rest, table, out_ref, piece, sems):
    group, size = some_ref.shape[0] - 1, piece.shape[0]
    start = some_ref.shape[1] - size
    rows = rest.shape[1] // size
    copies = [
        pltpu.make_async_copy(some_ref.at[:group], out_ref.at[:group], sems.at[0]),
        pltpu.make_async_copy(
            some_ref.at[group, pl.ds(0, start)], out_ref.at[group, pl.ds(0, start)], sems.at[1]
        ),
        pltpu.make_async_copy(piece, out_ref.at[group, pl.ds(start, size)], sems.at[2]),
    ]
    copies[0].start()
    copies[1].start()
    for shot in range(size):
        for strip in range(rest.shape[0]):
            piece[shot, strip * LANES : (strip + 1) * LANES, :] = inverse(
                rest[strip, shot * rows : (shot + 1) * rows], table[...]
            )
    copies[2].start()
    for copy in copies:
        copy.wait()


def kernel(
    chips, cores, mirror_hbm, surface_hbm, tables_hbm, records_ref, traces, rest, table_out,
    stage, send, held, left, block, first, totals, back, surface_ref, tables, mirror_ref,
    small_sems, load_sems, own_sems, send_sem, recv_sems, pass_sems, back_send_sem, back_recv_sems, entered,
):
    me = lax.axis_index("shot")
    core = lax.axis_index("pair")
    groups, parts, shots, width = send.shape[1:]
    freqs = parts // 2
    rows = chips * parts
    strips = width // LANES
    half = chips // 2
    quarter = chips // 4
    across = jnp.where(me < half, 0, 1)
    plane = me // quarter
    place = lax.rem(me, quarter)
    planes = (plane, plane + 1 - 2 * lax.rem(plane, 2), 3 * (1 - across), 2 - across)
    cuts = [cut(shots, group, groups) for group in range(groups)]

    def strip_of(strip):
        return slice(strip * LANES, (strip + 1) * LANES)

    def level(step):
        return plane * quarter + lax.rem(me + step, quarter)

    def upright(there):
        return there * quarter + place

    def peer(step):
        return lax.rem(core + step, cores)

    def flipped(there, flip):
        spot = place
        for bit in range(flip.bit_length()):
            if flip >> bit & 1:
                spot = spot + (1 << bit) - (2 << bit) * lax.rem(spot // (1 << bit), 2)
        return there * quarter + spot

    def load(group, some):
        return pltpu.make_async_copy(
            records_ref.at[group, some], traces.at[group, some], load_sems.at[group, int(some.start > 0)]
        )

    split = cuts[0][0][0][1]
    loads = [(0, pl.ds(0, split))]
    if split < shots:
        loads.append((0, pl.ds(split, shots - split)))
    loads.extend((group, pl.ds(0, shots)) for group in range(1, groups))
    for some in loads[:2]:
        load(*some).start()
    surface_copy = pltpu.make_async_copy(surface_hbm, surface_ref, small_sems.at[0])
    mirror_copy = pltpu.make_async_copy(mirror_hbm, mirror_ref, small_sems.at[1])
    tables_copy = pltpu.make_async_copy(tables_hbm, tables, small_sems.at[2])
    tables_copy.start()
    surface_copy.start()
    mirror_copy.start()

    barrier = pltpu.get_barrier_semaphore()

    @pl.loop(1, quarter)
    def _(step):
        pl.semaphore_signal(barrier, inc=1, device_id=(core, level(step)), device_id_type=MESH)

    for step in range(1, 4):
        pl.semaphore_signal(barrier, inc=1, device_id=(core, upright(planes[step])), device_id_type=MESH)
    for step in range(1, cores):
        pl.semaphore_signal(barrier, inc=1, device_id=(peer(step), me), device_id_type=MESH)

    def spread(source, target, group, some):
        return pltpu.make_async_remote_copy(
            src_ref=send.at[target, group, :, some],
            dst_ref=held.at[core, group, :, source, some],
            send_sem=send_sem,
            recv_sem=recv_sems.at[group, source // quarter],
            device_id=(core, target),
            device_id_type=MESH,
        )

    def arrived(group, there, count):
        some = held.at[core, group, :, pl.ds(0, count)]
        return pltpu.make_async_remote_copy(
            src_ref=some,
            dst_ref=some,
            send_sem=send_sem,
            recv_sem=recv_sems.at[group, there],
            device_id=(core, me),
            device_id_type=MESH,
        )

    def hand_on(some, other):
        return pltpu.make_async_remote_copy(
            src_ref=some,
            dst_ref=some,
            send_sem=pass_sems.at[other - 1, 0],
            recv_sem=pass_sems.at[other - 1, 1],
            device_id=(peer(other), me),
            device_id_type=MESH,
        )

    def keep(group):
        return pltpu.make_async_copy(
            send.at[me, group], held.at[core, group, :, me], own_sems.at[group]
        )

    def send_back(source, target, group, index):
        some = pl.ds(*cuts[group][1][index])
        return pltpu.make_async_remote_copy(
            src_ref=totals.at[target, group, :, some],
            dst_ref=back.at[source, group, :, some],
            send_sem=back_send_sem,
            recv_sem=back_recv_sems.at[group, index, source // quarter],
            device_id=(core, target),
            device_id_type=MESH,
        )

    def returned(group, index, there, count):
        some = back.at[pl.ds(0, count), group, :, pl.ds(*cuts[group][1][index])]
        return pltpu.make_async_remote_copy(
            src_ref=some,
            dst_ref=some,
            send_sem=back_send_sem,
            recv_sem=back_recv_sems.at[group, index, there],
            device_id=(core, me),
            device_id_type=MESH,
        )

    def sent(buffer, sem):
        some = buffer.at[pl.ds(0, chips - 1)]
        return pltpu.make_async_remote_copy(
            src_ref=some,
            dst_ref=some,
            send_sem=sem,
            recv_sem=recv_sems.at[0, 0],
            device_id=(core, me),
            device_id_type=MESH,
        )

    def to_level(there, start, last=0):
        for flip in range(quarter - 1, last - 1, -1):
            target = flipped(there, flip)
            if flip > 0:
                start(target)
            else:
                pl.when(target != me)(functools.partial(start, target))

    def spread_level(there, group):
        to_level(there, lambda target: spread(me, target, group, pl.ds(0, shots)).start(), int(group == 0))

    def spectra(group, index):
        start, size = cuts[group][0][index]
        for some in loads:
            if some[0] == group and some[1].start == start:
                load(*some).wait()
                if some == loads[0]:
                    for other in loads[2:]:
                        load(*other).start()
        for shot in range(start, start + size):
            value = lax.dot_general(
                tables[0], traces[group, shot], (((1,), (1,)), ((), ())),
                preferred_element_type=jnp.float32,
            )
            for strip in range(strips):
                stage[strip, shot * rows : (shot + 1) * rows] = value[:, strip_of(strip)]
        for row in range(rows):
            for strip in range(strips):
                value = stage[strip, pl.ds(start * rows + row, size, stride=rows), :]
                send[row // parts, group, row % parts, start : start + size, strip_of(strip)] = (
                    value.astype(jnp.bfloat16)
                )

    tables_copy.wait()
    for index, piece in enumerate(cuts[0][0]):
        spectra(0, index)
        if index == 0:
            pl.semaphore_wait(barrier, quarter + 2 + cores - 1)

            @pl.loop(1, quarter)
            def _(step):
                pl.semaphore_signal(entered, inc=1, device_id=(core, level(step)), device_id_type=MESH)

        for order in (3, 2, 1):
            spread(me, upright(planes[order]), 0, pl.ds(*piece)).start()
    keep(0).start()
    pl.semaphore_wait(entered, quarter - 1)
    for group in range(groups):
        if group > 0:
            spectra(group, 0)
            keep(group).start()
        spread_level(2 - across, group)
        spread_level(1 + across, group)
    for group in range(groups):
        spread_level(3 * (1 - across), group)
        spread_level(3 * across, group)

    if table_out is not None:
        table_out[...] = tables[1]
    surface_copy.wait()
    mirror_copy.wait()
    for group in range(groups):
        for order, there in enumerate(planes):
            if order == 0:
                keep(group).wait()
            arrived(group, there, quarter - 1 if order == 0 else quarter).wait_recv()
            for other in range(1, cores):
                hand_on(held.at[core, group, :, pl.ds(there * quarter, quarter)], other).start()
    for other in range(1, cores):
        hand_on(held.at[core], other).wait()

    def matrix(slot, group, part):
        value = held[slot, group, part].astype(jnp.float32)
        return value.reshape(chips * shots, width)

    tall = chips * shots
    span = 16 if chips % 16 == 0 else chips
    tile = width if width % 256 == 0 else 2 * width
    for group in range(groups):
        mate = mirror_ref[core * groups + group]
        mate_slot = mate // groups
        mate_group = lax.rem(mate, groups)
        for freq in range(freqs):
            scale = -surface_ref[pl.ds(freq, 1), :] / math.sqrt(2.0 * width)
            mate_re = matrix(mate_slot, mate_group, 2 * freq)
            mate_im = matrix(mate_slot, mate_group, 2 * freq + 1)
            block[:tall, :width] = mate_re.astype(jnp.bfloat16)
            block[tall:, width:] = mate_re.astype(jnp.bfloat16)
            block[:tall, width:] = mate_im.astype(jnp.bfloat16)
            block[tall:, :width] = (-mate_im).astype(jnp.bfloat16)
            for part in range(2):
                columns = slice(part * width, (part + 1) * width)
                value = matrix(core, group, 2 * freq + part)
                left[:, columns] = (value * scale).astype(jnp.bfloat16)
            for order in range(ORDERS):
                for top in range(0, chips, span):
                    band = slice(top * shots, (top + span) * shots)
                    pieces = []
                    for start in range(0, 2 * width, tile):
                        piece = jnp.dot(
                            left[band, :], block[:, start : start + tile],
                            preferred_element_type=jnp.float32,
                        )
                        if order > 0:
                            piece = piece + first[band, start : start + tile]
                        if order + 1 < ORDERS:
                            first[band, start : start + tile] = piece
                            pieces.append(piece)
                        else:
                            for low in range(start, start + tile, width):
                                total = piece[:, low - start : low - start + width]
                                totals[top : top + span, group, 2 * freq + low // width] = (
                                    total.reshape(span, shots, width).astype(jnp.bfloat16)
                                )
                    if order + 1 < ORDERS:
                        product = jnp.concatenate(pieces, axis=1) if len(pieces) > 1 else pieces[0]
                        wide = jnp.concatenate([scale, scale], axis=1)
                        left[band, :] = (product * wide).astype(jnp.bfloat16)

        ahead = (1 - across) * half
        pieces = range(len(cuts[group][1]))
        if group + 1 == groups:
            for index in pieces:
                send_back(me, ahead, group, index).start()
        for beyond in (True, False):
            for index in pieces:

                def start(target):
                    send = send_back(me, target, group, index).start
                    if beyond and group + 1 == groups:
                        pl.when(target != ahead)(send)
                    else:
                        send()

                low = 2 * (1 - across) if beyond else 2 * across
                to_level(low, start)
                to_level(low + 1, start)

    sent(send, send_sem).wait_send()

    for group in range(groups):
        for index, (start, size) in enumerate(cuts[group][1]):

            last = group + 1 == groups and index + 1 == len(cuts[group][1])
            there, offset = (rest, 0) if last and rest is not None else (stage, start)

            def unpack(buffer, source):
                for part in range(parts):
                    value = buffer[source, group, part, start : start + size].astype(jnp.float32)
                    row = offset * rows + source * parts + part
                    for strip in range(strips):
                        there[strip, pl.ds(row, size, stride=rows), :] = value[:, strip_of(strip)]

            unpack(totals, me)
            for order, away in enumerate(planes):
                returned(group, index, away, quarter if order else quarter - 1).wait_recv()

                @pl.loop(0 if order else 1, quarter)
                def _(step):
                    unpack(back, away * quarter + lax.rem(me + step, quarter))

            if there is not rest:
                for shot in range(start, start + size):
                    for strip in range(strips):
                        traces[group, shot, strip_of(strip), :] = inverse(
                            stage[strip, shot * rows : (shot + 1) * rows], tables[1]
                        )

    sent(totals, back_send_sem).wait_send()


def local(records, surface, mirror):
    chips = lax.axis_size("shot")
    cores = lax.axis_size("pair")
    groups, shots, receivers, time = records.shape
    freqs = surface.shape[0]
    parts = 2 * freqs
    tables = jnp.asarray(make_tables(freqs * chips, time))
    tall = chips * shots
    block_shape = (chips, groups, parts, shots, receivers)
    dma = pltpu.SemaphoreType.DMA
    scratch = [
        ((receivers // LANES, shots * chips * parts, LANES), jnp.float32),
        (block_shape, jnp.bfloat16),
        ((cores, groups, parts, chips, shots, receivers), jnp.bfloat16),
        ((tall, 2 * receivers), jnp.bfloat16),
        ((2 * tall, 2 * receivers), jnp.bfloat16),
        ((tall, 2 * receivers), jnp.float32),
        (block_shape, jnp.bfloat16),
        (block_shape, jnp.bfloat16),
    ]
    held_bytes = sum(math.prod(shape) * jnp.dtype(kind).itemsize for shape, kind in scratch)
    out_bytes = records.size * records.dtype.itemsize
    size = cut(shots, groups - 1, groups)[1][-1][1]
    roomy = held_bytes + 2 * out_bytes < 32 * 1024 * 1024 and size < shots
    grant = held_bytes + out_bytes + 8 * 1024 * 1024 if roomy else VMEM_BYTES
    hbm = pl.BlockSpec(memory_space=pltpu.HBM)
    vmem = pl.BlockSpec(memory_space=pltpu.VMEM)
    if roomy:
        rest_shape = (receivers // LANES, size * chips * parts, LANES)
        body = functools.partial(kernel, chips, cores)
        out_shape = [pltpu.VMEM(records.shape, jnp.bfloat16), pltpu.VMEM(rest_shape, jnp.float32)]
        out_shape.append(pltpu.VMEM(tables.shape[1:], tables.dtype))
        out_specs = [vmem] * 3
    else:
        def body(mirror_hbm, surface_hbm, tables_hbm, records_ref, out_ref, *others):
            kernel(chips, cores, mirror_hbm, surface_hbm, tables_hbm, records_ref, out_ref, None, None, *others)

        out_shape = jax.ShapeDtypeStruct(records.shape, jnp.bfloat16)
        out_specs = vmem
    result = pl.pallas_call(
        body,
        out_shape=out_shape,
        in_specs=[hbm] * 4,
        out_specs=out_specs,
        scratch_shapes=[
            *(pltpu.VMEM(shape, kind) for shape, kind in scratch),
            pltpu.VMEM(surface.shape, jnp.float32),
            pltpu.VMEM(tables.shape, tables.dtype),
            pltpu.SMEM(mirror.shape, jnp.int32),
            dma((3,)),
            dma((groups, 2)),
            dma((groups,)),
            dma,
            dma((groups, 4)),
            dma((max(cores - 1, 1), 2)),
            dma,
            dma((groups, 2, 4)),
            pltpu.SemaphoreType.REGULAR,
        ],
        compiler_params=pltpu.CompilerParams(
            collective_id=0, has_side_effects=True, vmem_limit_bytes=grant
        ),
    )(
        pltpu.with_memory_space_constraint(mirror, pltpu.HBM),
        pltpu.with_memory_space_constraint(surface, pltpu.HBM),
        pltpu.with_memory_space_constraint(tables, pltpu.HBM),
        pltpu.with_memory_space_constraint(records, pltpu.HBM),
    )
    if not roomy:
        return result
    piece = (size, receivers, time)
    return pl.pallas_call(
        finish,
        out_shape=jax.ShapeDtypeStruct(records.shape, jnp.bfloat16),
        in_specs=[pl.BlockSpec(memory_space=pl.ANY), vmem, vmem],
        out_specs=hbm,
        scratch_shapes=[pltpu.VMEM(piece, jnp.bfloat16), dma((3,))],
        compiler_params=pltpu.CompilerParams(
            vmem_limit_bytes=2 * math.prod(piece) + 4 * math.prod(rest_shape) + 2 * 1024 * 1024
        ),
    )(*result)


def solution(mesh):
    return jax.shard_map(
        local,
        mesh=mesh,
        in_specs=(P("pair", "shot", None, None), P("shot", None), P()),
        out_specs=P("pair", "shot", None, None),
        check_vma=False,
    )
```

```python
import functools
import math

import jax
import jax.numpy as jnp
import numpy as np
from jax import lax
from jax.experimental import pallas as pl
from jax.experimental.pallas import tpu as pltpu
from jax.sharding import PartitionSpec as P

ORDERS = 2
MESH = pl.DeviceIdType.MESH
VMEM_BYTES = 67043328
LANES = 128


def make_tables(freqs, time):
    row = np.arange(2 * freqs)[:, None]
    product = (row // 2 + 1) * np.arange(time)[None, :] % time
    phase = product.astype(np.float32) * np.float32(2.0 * math.pi / time)
    wave = np.where(row % 2 == 0, np.cos(phase), -np.sin(phase))
    forward = (wave * math.sqrt(2.0 / time)).astype(jnp.bfloat16)
    inverse = (wave / math.sqrt(freqs)).astype(jnp.bfloat16)
    return np.stack([forward, inverse])


def cut(shots, group, groups):
    whole = ((0, shots),)
    if shots % 8 or shots < 16:
        return whole, whole
    first = tuple((start, 8) for start in range(0, shots, 8)) if group == 0 else whole
    last = ((0, shots - 8), (shots - 8, 8)) if group + 1 == groups else whole
    return first, last


def inverse(value, table):
    total = lax.dot_general(
        value.astype(jnp.bfloat16), table, (((0,), (0,)), ((), ())),
        preferred_element_type=jnp.float32,
    )
    return total.astype(jnp.bfloat16)


def finish(some_ref, rest, table, out_ref, piece, sems):
    group, size = some_ref.shape[0] - 1, piece.shape[0]
    start = some_ref.shape[1] - size
    rows = rest.shape[1] // size
    copies = [
        pltpu.make_async_copy(some_ref.at[:group], out_ref.at[:group], sems.at[0]),
        pltpu.make_async_copy(
            some_ref.at[group, pl.ds(0, start)], out_ref.at[group, pl.ds(0, start)], sems.at[1]
        ),
        pltpu.make_async_copy(piece, out_ref.at[group, pl.ds(start, size)], sems.at[2]),
    ]
    copies[0].start()
    copies[1].start()
    for shot in range(size):
        for strip in range(rest.shape[0]):
            piece[shot, strip * LANES : (strip + 1) * LANES, :] = inverse(
                rest[strip, shot * rows : (shot + 1) * rows], table[...]
            )
    copies[2].start()
    for copy in copies:
        copy.wait()


def kernel(
    chips, cores, mirror_hbm, surface_hbm, tables_hbm, records_ref, traces, rest, table_out,
    stage, send, held, left, block, first, totals, back, surface_ref, tables, mirror_ref,
    small_sems, load_sems, own_sem, send_sem, recv_sems, pass_sems, back_send_sem, back_recv_sems, entered,
):
    me = lax.axis_index("shot")
    core = lax.axis_index("pair")
    groups, parts, shots, width = send.shape[1:]
    freqs = parts // 2
    rows = chips * parts
    strips = width // LANES
    half = chips // 2
    quarter = chips // 4
    across = jnp.where(me < half, 0, 1)
    plane = me // quarter
    middle = lax.rem(plane + 1, 4) // 2
    place = lax.rem(me, quarter)
    planes = (plane, plane + 1 - 2 * lax.rem(plane, 2), 3 * (1 - across), 2 - across)
    cuts = [cut(shots, group, groups) for group in range(groups)]

    def strip_of(strip):
        return slice(strip * LANES, (strip + 1) * LANES)

    def level(step):
        return plane * quarter + lax.rem(me + step, quarter)

    def upright(there):
        return there * quarter + place

    def peer(step):
        return lax.rem(core + step, cores)

    def flipped(there, flip):
        spot = place
        for bit in range(flip.bit_length()):
            if flip >> bit & 1:
                spot = spot + (1 << bit) - (2 << bit) * lax.rem(spot // (1 << bit), 2)
        return there * quarter + spot

    def load(group, some):
        return pltpu.make_async_copy(
            records_ref.at[group, some], traces.at[group, some], load_sems.at[group + int(group + some.start > 0)]
        )

    tables_copy = pltpu.make_async_copy(tables_hbm, tables, small_sems.at[2])
    tables_copy.start()
    split = cuts[0][0][0][1]
    loads = [(0, pl.ds(0, split))]
    if split < shots:
        loads.append((0, pl.ds(split, shots - split)))
    loads.extend((group, pl.ds(0, shots)) for group in range(1, groups))
    for some in loads[:2]:
        load(*some).start()
    surface_copy = pltpu.make_async_copy(surface_hbm, surface_ref, small_sems.at[0])
    mirror_copy = pltpu.make_async_copy(mirror_hbm, mirror_ref, small_sems.at[1])
    surface_copy.start()
    mirror_copy.start()

    barrier = pltpu.get_barrier_semaphore()

    @pl.loop(1, quarter)
    def _(step):
        pl.semaphore_signal(barrier, inc=1, device_id=(core, level(step)), device_id_type=MESH)

    for step in range(1, 4):
        pl.semaphore_signal(barrier, inc=1, device_id=(core, upright(planes[step])), device_id_type=MESH)
    for step in range(1, cores):
        pl.semaphore_signal(barrier, inc=1, device_id=(peer(step), me), device_id_type=MESH)

    def spread(source, target, group, some):
        return pltpu.make_async_remote_copy(
            src_ref=send.at[target, group, :, some],
            dst_ref=held.at[core, group, :, source, some],
            send_sem=send_sem,
            recv_sem=recv_sems.at[source // quarter],
            device_id=(core, target),
            device_id_type=MESH,
        )

    def arrived(there, count):
        some = held.at[core, :, :, pl.ds(0, count)]
        return pltpu.make_async_remote_copy(
            src_ref=some,
            dst_ref=some,
            send_sem=send_sem,
            recv_sem=recv_sems.at[there],
            device_id=(core, me),
            device_id_type=MESH,
        )

    def hand_on(some, other):
        return pltpu.make_async_remote_copy(
            src_ref=some,
            dst_ref=some,
            send_sem=pass_sems.at[other - 1, 0],
            recv_sem=pass_sems.at[other - 1, 1],
            device_id=(peer(other), me),
            device_id_type=MESH,
        )

    def keep():
        return pltpu.make_async_copy(send.at[me], held.at[core, :, :, me], own_sem)

    def batch(group, index, kind):
        return group + (3 * index + kind if group + 1 == groups else 0)

    def send_back(source, target, group, index):
        kind = jnp.where(target // half == across, 0, 1 + middle)
        some = pl.ds(*cuts[group][1][index])
        return pltpu.make_async_remote_copy(
            src_ref=totals.at[target, group, :, some],
            dst_ref=back.at[source, group, :, some],
            send_sem=back_send_sem,
            recv_sem=back_recv_sems.at[batch(group, index, kind)],
            device_id=(core, target),
            device_id_type=MESH,
        )

    def returned(group, index, kind, count):
        some = back.at[pl.ds(0, count), group, :, pl.ds(*cuts[group][1][index])]
        return pltpu.make_async_remote_copy(
            src_ref=some,
            dst_ref=some,
            send_sem=back_send_sem,
            recv_sem=back_recv_sems.at[batch(group, index, kind)],
            device_id=(core, me),
            device_id_type=MESH,
        )

    def sent(buffer, sem):
        some = buffer.at[pl.ds(0, chips - 1)]
        return pltpu.make_async_remote_copy(
            src_ref=some,
            dst_ref=some,
            send_sem=sem,
            recv_sem=recv_sems.at[0],
            device_id=(core, me),
            device_id_type=MESH,
        )

    def to_level(there, start, last=0):
        for flip in range(quarter - 1, last - 1, -1):
            target = flipped(there, flip)
            if flip > 0:
                start(target)
            else:
                pl.when(target != me)(functools.partial(start, target))

    def spread_level(there, group):
        to_level(there, lambda target: spread(me, target, group, pl.ds(0, shots)).start(), int(group == 0))

    def spectra(group, index):
        start, size = cuts[group][0][index]
        for some in loads:
            if some[0] == group and some[1].start == start:
                load(*some).wait()
                if some == loads[0]:
                    for other in loads[2:]:
                        load(*other).start()
        for shot in range(start, start + size):
            value = lax.dot_general(
                tables[0], traces[group, shot], (((1,), (1,)), ((), ())),
                preferred_element_type=jnp.float32,
            )
            for strip in range(strips):
                stage[strip, shot * rows : (shot + 1) * rows] = value[:, strip_of(strip)]
        for row in range(rows):
            for strip in range(strips):
                value = stage[strip, pl.ds(start * rows + row, size, stride=rows), :]
                send[row // parts, group, row % parts, start : start + size, strip_of(strip)] = (
                    value.astype(jnp.bfloat16)
                )

    tables_copy.wait()
    for index, piece in enumerate(cuts[0][0]):
        spectra(0, index)
        if index == 0:
            pl.semaphore_wait(barrier, quarter + 2 + cores - 1)

            @pl.loop(1, quarter)
            def _(step):
                pl.semaphore_signal(entered, inc=1, device_id=(core, level(step)), device_id_type=MESH)

        for order in (3, 2, 1):
            spread(me, upright(planes[order]), 0, pl.ds(*piece)).start()
    pl.semaphore_wait(entered, quarter - 1)
    for group in range(groups):
        if group > 0:
            spectra(group, 0)
        if group + 1 == groups:
            keep().start()
        spread_level(2 - across, group)
        spread_level(1 + across, group)
    for group in range(groups):
        spread_level(3 * (1 - across), group)
        spread_level(3 * across, group)

    if table_out is not None:
        table_out[...] = tables[1]
    surface_copy.wait()
    mirror_copy.wait()
    keep().wait()
    for order, there in enumerate(planes):
        arrived(there, quarter if order else quarter - 1).wait_recv()
        for other in range(1, cores):
            hand_on(held.at[core, :, :, pl.ds(there * quarter, quarter)], other).start()
    for other in range(1, cores):
        hand_on(held.at[core], other).wait()

    def matrix(slot, group, part):
        value = held[slot, group, part].astype(jnp.float32)
        return value.reshape(chips * shots, width)

    tall = chips * shots
    span = 16 if chips % 16 == 0 else chips
    tile = width if width % 256 == 0 else 2 * width
    for group in range(groups):
        mate = mirror_ref[core * groups + group]
        mate_slot = mate // groups
        mate_group = lax.rem(mate, groups)
        for freq in range(freqs):
            scale = -surface_ref[pl.ds(freq, 1), :] / math.sqrt(2.0 * width)
            mate_re = matrix(mate_slot, mate_group, 2 * freq)
            mate_im = matrix(mate_slot, mate_group, 2 * freq + 1)
            block[:tall, :width] = mate_re.astype(jnp.bfloat16)
            block[tall:, width:] = mate_re.astype(jnp.bfloat16)
            block[:tall, width:] = mate_im.astype(jnp.bfloat16)
            block[tall:, :width] = (-mate_im).astype(jnp.bfloat16)
            for part in range(2):
                columns = slice(part * width, (part + 1) * width)
                value = matrix(core, group, 2 * freq + part)
                left[:, columns] = (value * scale).astype(jnp.bfloat16)
            for order in range(ORDERS):
                for top in range(0, chips, span):
                    band = slice(top * shots, (top + span) * shots)
                    pieces = []
                    for start in range(0, 2 * width, tile):
                        piece = jnp.dot(
                            left[band, :], block[:, start : start + tile],
                            preferred_element_type=jnp.float32,
                        )
                        if order > 0:
                            piece = piece + first[band, start : start + tile]
                        if order + 1 < ORDERS:
                            first[band, start : start + tile] = piece
                            pieces.append(piece)
                        else:
                            for low in range(start, start + tile, width):
                                total = piece[:, low - start : low - start + width]
                                totals[top : top + span, group, 2 * freq + low // width] = (
                                    total.reshape(span, shots, width).astype(jnp.bfloat16)
                                )
                    if order + 1 < ORDERS:
                        product = jnp.concatenate(pieces, axis=1) if len(pieces) > 1 else pieces[0]
                        wide = jnp.concatenate([scale, scale], axis=1)
                        left[band, :] = (product * wide).astype(jnp.bfloat16)

        ahead = (1 - across) * half
        pieces = range(len(cuts[group][1]))
        if group + 1 == groups:
            for there in (ahead, ahead + quarter):
                for index in pieces:
                    send_back(me, there, group, index).start()
        for beyond in (True, False):
            for index in pieces:

                def start(target):
                    send = send_back(me, target, group, index).start
                    if beyond and group + 1 == groups:
                        pl.when(lax.rem(target, quarter) != 0)(send)
                    else:
                        send()

                low = 2 * (1 - across) if beyond else 2 * across
                to_level(low, start)
                to_level(low + 1, start)

    sent(send, send_sem).wait_send()

    for group in range(groups):
        for index, (start, size) in enumerate(cuts[group][1]):

            last = group + 1 == groups and index + 1 == len(cuts[group][1])
            there, offset = (rest, 0) if last and rest is not None else (stage, start)

            def unpack(buffer, source):
                for part in range(parts):
                    value = buffer[source, group, part, start : start + size].astype(jnp.float32)
                    row = offset * rows + source * parts + part
                    for strip in range(strips):
                        there[strip, pl.ds(row, size, stride=rows), :] = value[:, strip_of(strip)]

            unpack(totals, me)
            spans = [(across * half, half), (3 * (1 - across) * quarter, quarter), ((2 - across) * quarter, quarter)]
            if group + 1 < groups:
                spans = [(0, chips)]
            for kind, (base, count) in enumerate(spans):
                returned(group, index, kind, count - int(kind == 0)).wait_recv()

                @pl.loop(int(kind == 0), count)
                def _(step):
                    unpack(back, base + lax.rem(me + step, count))

            if there is not rest:
                for shot in range(start, start + size):
                    for strip in range(strips):
                        traces[group, shot, strip_of(strip), :] = inverse(
                            stage[strip, shot * rows : (shot + 1) * rows], tables[1]
                        )

    sent(totals, back_send_sem).wait_send()


def local(records, surface, mirror):
    chips = lax.axis_size("shot")
    cores = lax.axis_size("pair")
    groups, shots, receivers, time = records.shape
    freqs = surface.shape[0]
    parts = 2 * freqs
    tables = jnp.asarray(make_tables(freqs * chips, time))
    tall = chips * shots
    block_shape = (chips, groups, parts, shots, receivers)
    dma = pltpu.SemaphoreType.DMA
    scratch = [
        ((receivers // LANES, shots * chips * parts, LANES), jnp.float32),
        (block_shape, jnp.bfloat16),
        ((cores, groups, parts, chips, shots, receivers), jnp.bfloat16),
        ((tall, 2 * receivers), jnp.bfloat16),
        ((2 * tall, 2 * receivers), jnp.bfloat16),
        ((tall, 2 * receivers), jnp.float32),
        (block_shape, jnp.bfloat16),
        (block_shape, jnp.bfloat16),
    ]
    held_bytes = sum(math.prod(shape) * jnp.dtype(kind).itemsize for shape, kind in scratch)
    out_bytes = records.size * records.dtype.itemsize
    size = cut(shots, groups - 1, groups)[1][-1][1]
    roomy = held_bytes + 2 * out_bytes < 32 * 1024 * 1024 and size < shots
    grant = held_bytes + out_bytes + 8 * 1024 * 1024 if roomy else VMEM_BYTES
    hbm = pl.BlockSpec(memory_space=pltpu.HBM)
    vmem = pl.BlockSpec(memory_space=pltpu.VMEM)
    if roomy:
        rest_shape = (receivers // LANES, size * chips * parts, LANES)
        body = functools.partial(kernel, chips, cores)
        out_shape = [pltpu.VMEM(records.shape, jnp.bfloat16), pltpu.VMEM(rest_shape, jnp.float32)]
        out_shape.append(pltpu.VMEM(tables.shape[1:], tables.dtype))
        out_specs = [vmem] * 3
    else:
        def body(mirror_hbm, surface_hbm, tables_hbm, records_ref, out_ref, *others):
            kernel(chips, cores, mirror_hbm, surface_hbm, tables_hbm, records_ref, out_ref, None, None, *others)

        out_shape = jax.ShapeDtypeStruct(records.shape, jnp.bfloat16)
        out_specs = vmem
    result = pl.pallas_call(
        body,
        out_shape=out_shape,
        in_specs=[hbm] * 4,
        out_specs=out_specs,
        scratch_shapes=[
            *(pltpu.VMEM(shape, kind) for shape, kind in scratch),
            pltpu.VMEM(surface.shape, jnp.float32),
            pltpu.VMEM(tables.shape, tables.dtype),
            pltpu.SMEM(mirror.shape, jnp.int32),
            dma((3,)),
            dma((groups + 1,)),
            dma,
            dma,
            dma((4,)),
            dma((max(cores - 1, 1), 2)),
            dma,
            dma((groups + 5,)),
            pltpu.SemaphoreType.REGULAR,
        ],
        compiler_params=pltpu.CompilerParams(
            collective_id=0, has_side_effects=True, vmem_limit_bytes=grant
        ),
    )(
        pltpu.with_memory_space_constraint(mirror, pltpu.HBM),
        pltpu.with_memory_space_constraint(surface, pltpu.HBM),
        pltpu.with_memory_space_constraint(tables, pltpu.HBM),
        pltpu.with_memory_space_constraint(records, pltpu.HBM),
    )
    if not roomy:
        return result
    piece = (size, receivers, time)
    return pl.pallas_call(
        finish,
        out_shape=jax.ShapeDtypeStruct(records.shape, jnp.bfloat16),
        in_specs=[pl.BlockSpec(memory_space=pl.ANY), vmem, vmem],
        out_specs=hbm,
        scratch_shapes=[pltpu.VMEM(piece, jnp.bfloat16), dma((3,))],
        compiler_params=pltpu.CompilerParams(
            vmem_limit_bytes=2 * math.prod(piece) + 4 * math.prod(rest_shape) + 2 * 1024 * 1024
        ),
    )(*result)


def solution(mesh):
    return jax.shard_map(
        local,
        mesh=mesh,
        in_specs=(P("pair", "shot", None, None), P("shot", None), P()),
        out_specs=P("pair", "shot", None, None),
        check_vma=False,
    )
```

```python
import functools
import math

import jax
import jax.numpy as jnp
import numpy as np
from jax import lax
from jax.experimental import pallas as pl
from jax.experimental.pallas import tpu as pltpu
from jax.sharding import PartitionSpec as P

ORDERS = 2
MESH = pl.DeviceIdType.MESH
VMEM_BYTES = 67043328
LANES = 128


def make_tables(freqs, time):
    row = np.arange(2 * freqs)[:, None]
    product = (row // 2 + 1) * np.arange(time)[None, :] % time
    phase = product.astype(np.float32) * np.float32(2.0 * math.pi / time)
    wave = np.where(row % 2 == 0, np.cos(phase), -np.sin(phase))
    forward = (wave * math.sqrt(2.0 / time)).astype(jnp.bfloat16)
    inverse = (wave / math.sqrt(freqs)).astype(jnp.bfloat16)
    return np.stack([forward, inverse])


def cut(shots, group, groups):
    whole = ((0, shots),)
    if shots % 8 or shots < 16:
        return whole, whole
    first = tuple((start, 8) for start in range(0, shots, 8)) if group == 0 else whole
    last = ((0, 8), (8, shots - 8)) if group + 1 == groups else whole
    return first, last


def inverse(value, table):
    total = lax.dot_general(
        value.astype(jnp.bfloat16), table, (((0,), (0,)), ((), ())),
        preferred_element_type=jnp.float32,
    )
    return total.astype(jnp.bfloat16)


def finish(some_ref, rest, table, out_ref, piece, sems):
    group, size = some_ref.shape[0] - 1, piece.shape[0]
    start = some_ref.shape[1] - size
    rows = rest.shape[1] // size
    copies = [
        pltpu.make_async_copy(some_ref.at[:group], out_ref.at[:group], sems.at[0]),
        pltpu.make_async_copy(
            some_ref.at[group, pl.ds(0, start)], out_ref.at[group, pl.ds(0, start)], sems.at[1]
        ),
        pltpu.make_async_copy(piece, out_ref.at[group, pl.ds(start, size)], sems.at[2]),
    ]
    copies[0].start()
    copies[1].start()
    for shot in range(size):
        for strip in range(rest.shape[0]):
            piece[shot, strip * LANES : (strip + 1) * LANES, :] = inverse(
                rest[strip, shot * rows : (shot + 1) * rows], table[...]
            )
    copies[2].start()
    for copy in copies:
        copy.wait()


def kernel(
    chips, cores, mirror_hbm, surface_hbm, tables_hbm, records_ref, traces, rest, table_out,
    stage, send, held, left, block, first, totals, back, surface_ref, tables, mirror_ref,
    small_sems, load_sems, own_sem, send_sem, recv_sems, pass_sems, back_send_sem, back_recv_sems, entered,
):
    me = lax.axis_index("shot")
    core = lax.axis_index("pair")
    groups, parts, shots, width = send.shape[1:]
    freqs = parts // 2
    rows = chips * parts
    strips = width // LANES
    half = chips // 2
    quarter = chips // 4
    across = jnp.where(me < half, 0, 1)
    plane = me // quarter
    middle = lax.rem(plane + 1, 4) // 2
    place = lax.rem(me, quarter)
    planes = (plane, plane + 1 - 2 * lax.rem(plane, 2), 3 * (1 - across), 2 - across)
    cuts = [cut(shots, group, groups) for group in range(groups)]

    def strip_of(strip):
        return slice(strip * LANES, (strip + 1) * LANES)

    def level(step):
        return plane * quarter + lax.rem(me + step, quarter)

    def upright(there):
        return there * quarter + place

    def peer(step):
        return lax.rem(core + step, cores)

    def flipped(there, flip):
        spot = place
        for bit in range(flip.bit_length()):
            if flip >> bit & 1:
                spot = spot + (1 << bit) - (2 << bit) * lax.rem(spot // (1 << bit), 2)
        return there * quarter + spot

    def load(group, some):
        return pltpu.make_async_copy(
            records_ref.at[group, some], traces.at[group, some], load_sems.at[group + int(group + some.start > 0)]
        )

    tables_copy = pltpu.make_async_copy(tables_hbm, tables, small_sems.at[2])
    tables_copy.start()
    split = cuts[0][0][0][1]
    loads = [(0, pl.ds(0, split))]
    if split < shots:
        loads.append((0, pl.ds(split, shots - split)))
    loads.extend((group, pl.ds(0, shots)) for group in range(1, groups))
    for some in loads[:2]:
        load(*some).start()
    surface_copy = pltpu.make_async_copy(surface_hbm, surface_ref, small_sems.at[0])
    mirror_copy = pltpu.make_async_copy(mirror_hbm, mirror_ref, small_sems.at[1])
    surface_copy.start()
    mirror_copy.start()

    barrier = pltpu.get_barrier_semaphore()

    @pl.loop(1, quarter)
    def _(step):
        pl.semaphore_signal(barrier, inc=1, device_id=(core, level(step)), device_id_type=MESH)

    for step in range(1, 4):
        pl.semaphore_signal(barrier, inc=1, device_id=(core, upright(planes[step])), device_id_type=MESH)
    for step in range(1, cores):
        pl.semaphore_signal(barrier, inc=1, device_id=(peer(step), me), device_id_type=MESH)

    def spread(source, target, group, some):
        return pltpu.make_async_remote_copy(
            src_ref=send.at[target, group, :, some],
            dst_ref=held.at[core, group, :, source, some],
            send_sem=send_sem,
            recv_sem=recv_sems.at[source // quarter],
            device_id=(core, target),
            device_id_type=MESH,
        )

    def arrived(there, count):
        some = held.at[core, :, :, pl.ds(0, count)]
        return pltpu.make_async_remote_copy(
            src_ref=some,
            dst_ref=some,
            send_sem=send_sem,
            recv_sem=recv_sems.at[there],
            device_id=(core, me),
            device_id_type=MESH,
        )

    def hand_on(some, other):
        return pltpu.make_async_remote_copy(
            src_ref=some,
            dst_ref=some,
            send_sem=pass_sems.at[other - 1, 0],
            recv_sem=pass_sems.at[other - 1, 1],
            device_id=(peer(other), me),
            device_id_type=MESH,
        )

    def keep():
        return pltpu.make_async_copy(send.at[me], held.at[core, :, :, me], own_sem)

    def batch(group, index, kind):
        return group + (3 * index + kind if group + 1 == groups else 0)

    def send_back(source, target, group, index):
        kind = jnp.where(target // half == across, 0, 1 + middle)
        some = pl.ds(*cuts[group][1][index])
        return pltpu.make_async_remote_copy(
            src_ref=totals.at[target, group, :, some],
            dst_ref=back.at[source, group, :, some],
            send_sem=back_send_sem,
            recv_sem=back_recv_sems.at[batch(group, index, kind)],
            device_id=(core, target),
            device_id_type=MESH,
        )

    def returned(group, index, kind, count):
        some = back.at[pl.ds(0, count), group, :, pl.ds(*cuts[group][1][index])]
        return pltpu.make_async_remote_copy(
            src_ref=some,
            dst_ref=some,
            send_sem=back_send_sem,
            recv_sem=back_recv_sems.at[batch(group, index, kind)],
            device_id=(core, me),
            device_id_type=MESH,
        )

    def sent(buffer, sem):
        some = buffer.at[pl.ds(0, chips - 1)]
        return pltpu.make_async_remote_copy(
            src_ref=some,
            dst_ref=some,
            send_sem=sem,
            recv_sem=recv_sems.at[0],
            device_id=(core, me),
            device_id_type=MESH,
        )

    def to_level(there, start, last=0):
        for flip in range(quarter - 1, last - 1, -1):
            target = flipped(there, flip)
            if flip > 0:
                start(target)
            else:
                pl.when(target != me)(functools.partial(start, target))

    def spread_level(there, group):
        to_level(there, lambda target: spread(me, target, group, pl.ds(0, shots)).start(), int(group == 0))

    def spectra(group, index):
        start, size = cuts[group][0][index]
        for some in loads:
            if some[0] == group and some[1].start == start:
                load(*some).wait()
                if some == loads[0]:
                    for other in loads[2:]:
                        load(*other).start()
        for shot in range(start, start + size):
            value = lax.dot_general(
                tables[0], traces[group, shot], (((1,), (1,)), ((), ())),
                preferred_element_type=jnp.float32,
            )
            for strip in range(strips):
                stage[strip, shot * rows : (shot + 1) * rows] = value[:, strip_of(strip)]
        for row in range(rows):
            for strip in range(strips):
                value = stage[strip, pl.ds(start * rows + row, size, stride=rows), :]
                send[row // parts, group, row % parts, start : start + size, strip_of(strip)] = (
                    value.astype(jnp.bfloat16)
                )

    tables_copy.wait()
    for index, piece in enumerate(cuts[0][0]):
        spectra(0, index)
        if index == 0:
            pl.semaphore_wait(barrier, quarter + 2 + cores - 1)

            @pl.loop(1, quarter)
            def _(step):
                pl.semaphore_signal(entered, inc=1, device_id=(core, level(step)), device_id_type=MESH)

        for order in (3, 2, 1):
            spread(me, upright(planes[order]), 0, pl.ds(*piece)).start()
    pl.semaphore_wait(entered, quarter - 1)
    for group in range(groups):
        if group > 0:
            spectra(group, 0)
        if group + 1 == groups:
            keep().start()
        spread_level(2 - across, group)
        spread_level(1 + across, group)
    for group in range(groups):
        spread_level(3 * (1 - across), group)
        spread_level(3 * across, group)

    if table_out is not None:
        table_out[...] = tables[1]
    surface_copy.wait()
    mirror_copy.wait()
    keep().wait()
    for order, there in enumerate(planes):
        arrived(there, quarter if order else quarter - 1).wait_recv()
        for other in range(1, cores):
            hand_on(held.at[core, :, :, pl.ds(there * quarter, quarter)], other).start()
    for other in range(1, cores):
        hand_on(held.at[core], other).wait()

    def matrix(slot, group, part):
        value = held[slot, group, part].astype(jnp.float32)
        return value.reshape(chips * shots, width)

    tall = chips * shots
    span = 16 if chips % 16 == 0 else chips
    tile = width if width % 256 == 0 else 2 * width
    for group in range(groups):
        mate = mirror_ref[core * groups + group]
        mate_slot = mate // groups
        mate_group = lax.rem(mate, groups)
        for freq in range(freqs):
            scale = -surface_ref[pl.ds(freq, 1), :] / math.sqrt(2.0 * width)
            mate_re = matrix(mate_slot, mate_group, 2 * freq)
            mate_im = matrix(mate_slot, mate_group, 2 * freq + 1)
            block[:tall, :width] = mate_re.astype(jnp.bfloat16)
            block[tall:, width:] = mate_re.astype(jnp.bfloat16)
            block[:tall, width:] = mate_im.astype(jnp.bfloat16)
            block[tall:, :width] = (-mate_im).astype(jnp.bfloat16)
            for part in range(2):
                columns = slice(part * width, (part + 1) * width)
                value = matrix(core, group, 2 * freq + part)
                left[:, columns] = (value * scale).astype(jnp.bfloat16)
            for order in range(ORDERS):
                for top in range(0, chips, span):
                    band = slice(top * shots, (top + span) * shots)
                    pieces = []
                    for start in range(0, 2 * width, tile):
                        piece = jnp.dot(
                            left[band, :], block[:, start : start + tile],
                            preferred_element_type=jnp.float32,
                        )
                        if order > 0:
                            piece = piece + first[band, start : start + tile]
                        if order + 1 < ORDERS:
                            first[band, start : start + tile] = piece
                            pieces.append(piece)
                        else:
                            for low in range(start, start + tile, width):
                                total = piece[:, low - start : low - start + width]
                                totals[top : top + span, group, 2 * freq + low // width] = (
                                    total.reshape(span, shots, width).astype(jnp.bfloat16)
                                )
                    if order + 1 < ORDERS:
                        product = jnp.concatenate(pieces, axis=1) if len(pieces) > 1 else pieces[0]
                        wide = jnp.concatenate([scale, scale], axis=1)
                        left[band, :] = (product * wide).astype(jnp.bfloat16)

        beyond = (1 - across) * half
        pieces = range(len(cuts[group][1]))

        def rest_of(index):
            for step in range(2):
                to_level(
                    2 * (1 - across) + step,
                    lambda target: pl.when(lax.rem(target, quarter) != 0)(
                        send_back(me, target, group, index).start
                    ),
                )

        firsts = [0, quarter]
        if group + 1 == groups and len(pieces) > 1:
            for index in pieces:
                for spot in firsts:
                    send_back(me, beyond + spot, group, index).start()
            rest_of(0)
            rest_of(1)
        else:
            for index in pieces:
                for step in range(2):
                    to_level(2 * (1 - across) + step, lambda target: send_back(me, target, group, index).start())
        for index in pieces:
            for step in range(2):
                to_level(2 * across + step, lambda target: send_back(me, target, group, index).start())

    sent(send, send_sem).wait_send()

    for group in range(groups):
        for index, (start, size) in enumerate(cuts[group][1]):

            last = group + 1 == groups and index + 1 == len(cuts[group][1])
            there, offset = (rest, 0) if last and rest is not None else (stage, start)

            def unpack(buffer, source):
                for part in range(parts):
                    value = buffer[source, group, part, start : start + size].astype(jnp.float32)
                    row = offset * rows + source * parts + part
                    for strip in range(strips):
                        there[strip, pl.ds(row, size, stride=rows), :] = value[:, strip_of(strip)]

            unpack(totals, me)
            spans = [(across * half, half), (3 * (1 - across) * quarter, quarter), ((2 - across) * quarter, quarter)]
            if group + 1 < groups:
                spans = [(0, chips)]
            for kind, (base, count) in enumerate(spans):
                returned(group, index, kind, count - int(kind == 0)).wait_recv()

                @pl.loop(int(kind == 0), count)
                def _(step):
                    unpack(back, base + lax.rem(me + step, count))

            if there is not rest:
                for shot in range(start, start + size):
                    for strip in range(strips):
                        traces[group, shot, strip_of(strip), :] = inverse(
                            stage[strip, shot * rows : (shot + 1) * rows], tables[1]
                        )

    sent(totals, back_send_sem).wait_send()


def local(records, surface, mirror):
    chips = lax.axis_size("shot")
    cores = lax.axis_size("pair")
    groups, shots, receivers, time = records.shape
    freqs = surface.shape[0]
    parts = 2 * freqs
    tables = jnp.asarray(make_tables(freqs * chips, time))
    tall = chips * shots
    block_shape = (chips, groups, parts, shots, receivers)
    dma = pltpu.SemaphoreType.DMA
    scratch = [
        ((receivers // LANES, shots * chips * parts, LANES), jnp.float32),
        (block_shape, jnp.bfloat16),
        ((cores, groups, parts, chips, shots, receivers), jnp.bfloat16),
        ((tall, 2 * receivers), jnp.bfloat16),
        ((2 * tall, 2 * receivers), jnp.bfloat16),
        ((tall, 2 * receivers), jnp.float32),
        (block_shape, jnp.bfloat16),
        (block_shape, jnp.bfloat16),
    ]
    held_bytes = sum(math.prod(shape) * jnp.dtype(kind).itemsize for shape, kind in scratch)
    out_bytes = records.size * records.dtype.itemsize
    size = cut(shots, groups - 1, groups)[1][-1][1]
    roomy = held_bytes + 2 * out_bytes < 32 * 1024 * 1024 and size < shots
    grant = held_bytes + out_bytes + 8 * 1024 * 1024 if roomy else VMEM_BYTES
    hbm = pl.BlockSpec(memory_space=pltpu.HBM)
    vmem = pl.BlockSpec(memory_space=pltpu.VMEM)
    if roomy:
        rest_shape = (receivers // LANES, size * chips * parts, LANES)
        body = functools.partial(kernel, chips, cores)
        out_shape = [pltpu.VMEM(records.shape, jnp.bfloat16), pltpu.VMEM(rest_shape, jnp.float32)]
        out_shape.append(pltpu.VMEM(tables.shape[1:], tables.dtype))
        out_specs = [vmem] * 3
    else:
        def body(mirror_hbm, surface_hbm, tables_hbm, records_ref, out_ref, *others):
            kernel(chips, cores, mirror_hbm, surface_hbm, tables_hbm, records_ref, out_ref, None, None, *others)

        out_shape = jax.ShapeDtypeStruct(records.shape, jnp.bfloat16)
        out_specs = vmem
    result = pl.pallas_call(
        body,
        out_shape=out_shape,
        in_specs=[hbm] * 4,
        out_specs=out_specs,
        scratch_shapes=[
            *(pltpu.VMEM(shape, kind) for shape, kind in scratch),
            pltpu.VMEM(surface.shape, jnp.float32),
            pltpu.VMEM(tables.shape, tables.dtype),
            pltpu.SMEM(mirror.shape, jnp.int32),
            dma((3,)),
            dma((groups + 1,)),
            dma,
            dma,
            dma((4,)),
            dma((max(cores - 1, 1), 2)),
            dma,
            dma((groups + 5,)),
            pltpu.SemaphoreType.REGULAR,
        ],
        compiler_params=pltpu.CompilerParams(
            collective_id=0, has_side_effects=True, vmem_limit_bytes=grant
        ),
    )(
        pltpu.with_memory_space_constraint(mirror, pltpu.HBM),
        pltpu.with_memory_space_constraint(surface, pltpu.HBM),
        pltpu.with_memory_space_constraint(tables, pltpu.HBM),
        pltpu.with_memory_space_constraint(records, pltpu.HBM),
    )
    if not roomy:
        return result
    piece = (size, receivers, time)
    return pl.pallas_call(
        finish,
        out_shape=jax.ShapeDtypeStruct(records.shape, jnp.bfloat16),
        in_specs=[pl.BlockSpec(memory_space=pl.ANY), vmem, vmem],
        out_specs=hbm,
        scratch_shapes=[pltpu.VMEM(piece, jnp.bfloat16), dma((3,))],
        compiler_params=pltpu.CompilerParams(
            vmem_limit_bytes=2 * math.prod(piece) + 4 * math.prod(rest_shape) + 2 * 1024 * 1024
        ),
    )(*result)


def solution(mesh):
    return jax.shard_map(
        local,
        mesh=mesh,
        in_specs=(P("pair", "shot", None, None), P("shot", None), P()),
        out_specs=P("pair", "shot", None, None),
        check_vma=False,
    )
```

```python
import functools
import math

import jax
import jax.numpy as jnp
import numpy as np
from jax import lax
from jax.experimental import pallas as pl
from jax.experimental.pallas import tpu as pltpu
from jax.sharding import PartitionSpec as P

ORDERS = 2
MESH = pl.DeviceIdType.MESH
VMEM_BYTES = 67043328
LANES = 128


def make_tables(freqs, time):
    row = np.arange(2 * freqs)[:, None]
    product = (row // 2 + 1) * np.arange(time)[None, :] % time
    phase = product.astype(np.float32) * np.float32(2.0 * math.pi / time)
    wave = np.where(row % 2 == 0, np.cos(phase), -np.sin(phase))
    forward = (wave * math.sqrt(2.0 / time)).astype(jnp.bfloat16)
    inverse = (wave / math.sqrt(freqs)).astype(jnp.bfloat16)
    return np.stack([forward, inverse])


def cut(shots, group, groups):
    whole = ((0, shots),)
    if shots % 8 or shots < 16:
        return whole, whole
    first = tuple((start, 8) for start in range(0, shots, 8)) if group == 0 else whole
    last = ((0, 8), (8, shots - 8)) if group + 1 == groups else whole
    return first, last


def inverse(value, table):
    total = lax.dot_general(
        value.astype(jnp.bfloat16), table, (((0,), (0,)), ((), ())),
        preferred_element_type=jnp.float32,
    )
    return total.astype(jnp.bfloat16)


def finish(some_ref, rest, table, out_ref, piece, sems):
    group, size = some_ref.shape[0] - 1, piece.shape[0]
    start = some_ref.shape[1] - size
    rows = rest.shape[1] // size
    copies = [pltpu.make_async_copy(some_ref.at[:group], out_ref.at[:group], sems.at[0])]
    if start > 0:
        copies.append(
            pltpu.make_async_copy(
                some_ref.at[group, pl.ds(0, start)], out_ref.at[group, pl.ds(0, start)], sems.at[1]
            )
        )
    for copy in copies:
        copy.start()
    chunk = 8 if size % 8 == 0 else size
    for low in range(0, size, chunk):
        for shot in range(low, low + chunk):
            for strip in range(rest.shape[0]):
                piece[shot, strip * LANES : (strip + 1) * LANES, :] = inverse(
                    rest[strip, shot * rows : (shot + 1) * rows], table[...]
                )
        copies.append(
            pltpu.make_async_copy(
                piece.at[pl.ds(low, chunk)],
                out_ref.at[group, pl.ds(start + low, chunk)],
                sems.at[2 + low // chunk],
            )
        )
        copies[-1].start()
    for copy in copies:
        copy.wait()


def kernel(
    chips, cores, mirror_hbm, surface_hbm, tables_hbm, records_ref, traces, rest, table_out,
    stage, send, held, left, block, first, totals, back, surface_ref, tables, mirror_ref,
    small_sems, load_sems, own_sem, send_sem, recv_sems, pass_sems, back_send_sem, back_recv_sems, entered,
):
    me = lax.axis_index("shot")
    core = lax.axis_index("pair")
    groups, parts, shots, width = send.shape[1:]
    freqs = parts // 2
    rows = chips * parts
    strips = width // LANES
    half = chips // 2
    quarter = chips // 4
    across = jnp.where(me < half, 0, 1)
    plane = me // quarter
    middle = lax.rem(plane + 1, 4) // 2
    place = lax.rem(me, quarter)
    planes = (plane, plane + 1 - 2 * lax.rem(plane, 2), 3 * (1 - across), 2 - across)
    cuts = [cut(shots, group, groups) for group in range(groups)]

    def strip_of(strip):
        return slice(strip * LANES, (strip + 1) * LANES)

    def level(step):
        return plane * quarter + lax.rem(me + step, quarter)

    def upright(there):
        return there * quarter + place

    def peer(step):
        return lax.rem(core + step, cores)

    def flipped(there, flip):
        spot = place
        for bit in range(flip.bit_length()):
            if flip >> bit & 1:
                spot = spot + (1 << bit) - (2 << bit) * lax.rem(spot // (1 << bit), 2)
        return there * quarter + spot

    split = cuts[0][0][0][1]
    bit = 4 if split % 4 == 0 else split
    loads = [(0, pl.ds(start, bit)) for start in range(0, split, bit)]
    head = len(loads)
    if split < shots:
        loads.append((0, pl.ds(split, shots - split)))
    loads.extend((group, pl.ds(0, shots)) for group in range(1, groups))

    def load(index):
        group, some = loads[index]
        return pltpu.make_async_copy(
            records_ref.at[group, some], traces.at[group, some], load_sems.at[index]
        )

    tables_copy = pltpu.make_async_copy(tables_hbm, tables, small_sems.at[2])
    tables_copy.start()
    for index in range(head + int(split < shots)):
        load(index).start()
    surface_copy = pltpu.make_async_copy(surface_hbm, surface_ref, small_sems.at[0])
    mirror_copy = pltpu.make_async_copy(mirror_hbm, mirror_ref, small_sems.at[1])
    surface_copy.start()
    mirror_copy.start()

    barrier = pltpu.get_barrier_semaphore()

    @pl.loop(1, quarter)
    def _(step):
        pl.semaphore_signal(barrier, inc=1, device_id=(core, level(step)), device_id_type=MESH)

    for step in range(1, 4):
        pl.semaphore_signal(barrier, inc=1, device_id=(core, upright(planes[step])), device_id_type=MESH)
    for step in range(1, cores):
        pl.semaphore_signal(barrier, inc=1, device_id=(peer(step), me), device_id_type=MESH)

    def spread(source, target, group, some):
        return pltpu.make_async_remote_copy(
            src_ref=send.at[target, group, :, some],
            dst_ref=held.at[core, group, :, source, some],
            send_sem=send_sem,
            recv_sem=recv_sems.at[source // quarter],
            device_id=(core, target),
            device_id_type=MESH,
        )

    def arrived(there, count):
        some = held.at[core, :, :, pl.ds(0, count)]
        return pltpu.make_async_remote_copy(
            src_ref=some,
            dst_ref=some,
            send_sem=send_sem,
            recv_sem=recv_sems.at[there],
            device_id=(core, me),
            device_id_type=MESH,
        )

    def hand_on(some, other):
        return pltpu.make_async_remote_copy(
            src_ref=some,
            dst_ref=some,
            send_sem=pass_sems.at[other - 1, 0],
            recv_sem=pass_sems.at[other - 1, 1],
            device_id=(peer(other), me),
            device_id_type=MESH,
        )

    def keep():
        return pltpu.make_async_copy(send.at[me], held.at[core, :, :, me], own_sem)

    def batch(group, index, kind):
        return group + (3 * index + kind if group + 1 == groups else 0)

    def send_back(source, target, group, index):
        kind = jnp.where(target // half == across, 0, 1 + middle)
        some = pl.ds(*cuts[group][1][index])
        return pltpu.make_async_remote_copy(
            src_ref=totals.at[target, group, :, some],
            dst_ref=back.at[source, group, :, some],
            send_sem=back_send_sem,
            recv_sem=back_recv_sems.at[batch(group, index, kind)],
            device_id=(core, target),
            device_id_type=MESH,
        )

    def returned(group, index, kind, count):
        some = back.at[pl.ds(0, count), group, :, pl.ds(*cuts[group][1][index])]
        return pltpu.make_async_remote_copy(
            src_ref=some,
            dst_ref=some,
            send_sem=back_send_sem,
            recv_sem=back_recv_sems.at[batch(group, index, kind)],
            device_id=(core, me),
            device_id_type=MESH,
        )

    def sent(buffer, sem):
        some = buffer.at[pl.ds(0, chips - 1)]
        return pltpu.make_async_remote_copy(
            src_ref=some,
            dst_ref=some,
            send_sem=sem,
            recv_sem=recv_sems.at[0],
            device_id=(core, me),
            device_id_type=MESH,
        )

    def to_level(there, start, last=0):
        for flip in range(quarter - 1, last - 1, -1):
            target = flipped(there, flip)
            if flip > 0:
                start(target)
            else:
                pl.when(target != me)(functools.partial(start, target))

    def spread_level(there, group):
        to_level(there, lambda target: spread(me, target, group, pl.ds(0, shots)).start(), int(group == 0))

    def spectra(group, index):
        start, size = cuts[group][0][index]
        for shot in range(start, start + size):
            for number, (whose, some) in enumerate(loads):
                if whose == group and some.start == shot:
                    load(number).wait()
                    if number == head - 1:
                        for other in range(head + int(split < shots), len(loads)):
                            load(other).start()
            value = lax.dot_general(
                tables[0], traces[group, shot], (((1,), (1,)), ((), ())),
                preferred_element_type=jnp.float32,
            )
            for strip in range(strips):
                stage[strip, shot * rows : (shot + 1) * rows] = value[:, strip_of(strip)]
        for row in range(rows):
            for strip in range(strips):
                value = stage[strip, pl.ds(start * rows + row, size, stride=rows), :]
                send[row // parts, group, row % parts, start : start + size, strip_of(strip)] = (
                    value.astype(jnp.bfloat16)
                )

    tables_copy.wait()
    for index, piece in enumerate(cuts[0][0]):
        spectra(0, index)
        if index == 0:
            pl.semaphore_wait(barrier, quarter + 2 + cores - 1)

            @pl.loop(1, quarter)
            def _(step):
                pl.semaphore_signal(entered, inc=1, device_id=(core, level(step)), device_id_type=MESH)

        for order in (3, 2, 1):
            spread(me, upright(planes[order]), 0, pl.ds(*piece)).start()
    pl.semaphore_wait(entered, quarter - 1)
    for group in range(groups):
        if group > 0:
            spectra(group, 0)
        if group + 1 == groups:
            keep().start()
        spread_level(2 - across, group)
        spread_level(1 + across, group)
    for group in range(groups):
        spread_level(3 * (1 - across), group)
        spread_level(3 * across, group)

    if table_out is not None:
        table_out[...] = tables[1]
    surface_copy.wait()
    mirror_copy.wait()
    keep().wait()
    for order, there in enumerate(planes):
        arrived(there, quarter if order else quarter - 1).wait_recv()
        for other in range(1, cores):
            hand_on(held.at[core, :, :, pl.ds(there * quarter, quarter)], other).start()
    for other in range(1, cores):
        hand_on(held.at[core], other).wait()

    def matrix(slot, group, part):
        value = held[slot, group, part].astype(jnp.float32)
        return value.reshape(chips * shots, width)

    tall = chips * shots
    span = 16 if chips % 16 == 0 else chips
    tile = width if width % 256 == 0 else 2 * width
    for group in range(groups):
        mate = mirror_ref[core * groups + group]
        mate_slot = mate // groups
        mate_group = lax.rem(mate, groups)
        for freq in range(freqs):
            scale = -surface_ref[pl.ds(freq, 1), :] / math.sqrt(2.0 * width)
            mate_re = matrix(mate_slot, mate_group, 2 * freq)
            mate_im = matrix(mate_slot, mate_group, 2 * freq + 1)
            block[:tall, :width] = mate_re.astype(jnp.bfloat16)
            block[tall:, width:] = mate_re.astype(jnp.bfloat16)
            block[:tall, width:] = mate_im.astype(jnp.bfloat16)
            block[tall:, :width] = (-mate_im).astype(jnp.bfloat16)
            for part in range(2):
                columns = slice(part * width, (part + 1) * width)
                value = matrix(core, group, 2 * freq + part)
                left[:, columns] = (value * scale).astype(jnp.bfloat16)
            for order in range(ORDERS):
                for top in range(0, chips, span):
                    band = slice(top * shots, (top + span) * shots)
                    pieces = []
                    for start in range(0, 2 * width, tile):
                        piece = jnp.dot(
                            left[band, :], block[:, start : start + tile],
                            preferred_element_type=jnp.float32,
                        )
                        if order > 0:
                            piece = piece + first[band, start : start + tile]
                        if order + 1 < ORDERS:
                            first[band, start : start + tile] = piece
                            pieces.append(piece)
                        else:
                            for low in range(start, start + tile, width):
                                total = piece[:, low - start : low - start + width]
                                totals[top : top + span, group, 2 * freq + low // width] = (
                                    total.reshape(span, shots, width).astype(jnp.bfloat16)
                                )
                    if order + 1 < ORDERS:
                        product = jnp.concatenate(pieces, axis=1) if len(pieces) > 1 else pieces[0]
                        wide = jnp.concatenate([scale, scale], axis=1)
                        left[band, :] = (product * wide).astype(jnp.bfloat16)

        beyond = (1 - across) * half
        pieces = range(len(cuts[group][1]))

        def rest_of(index):
            for step in range(2):
                to_level(
                    2 * (1 - across) + step,
                    lambda target: pl.when(lax.rem(target, quarter) != 0)(
                        send_back(me, target, group, index).start
                    ),
                )

        firsts = [0, quarter]
        if group + 1 == groups and len(pieces) > 1:
            for index in pieces:
                for spot in firsts:
                    send_back(me, beyond + spot, group, index).start()
            rest_of(0)
            rest_of(1)
        else:
            for index in pieces:
                for step in range(2):
                    to_level(2 * (1 - across) + step, lambda target: send_back(me, target, group, index).start())
        for index in pieces:
            for step in range(2):
                to_level(2 * across + step, lambda target: send_back(me, target, group, index).start())

    sent(send, send_sem).wait_send()

    for group in range(groups):
        for index, (start, size) in enumerate(cuts[group][1]):

            last = group + 1 == groups and index + 1 == len(cuts[group][1])
            there, offset = (rest, 0) if last and rest is not None else (stage, start)

            def unpack(buffer, source):
                for part in range(parts):
                    value = buffer[source, group, part, start : start + size].astype(jnp.float32)
                    row = offset * rows + source * parts + part
                    for strip in range(strips):
                        there[strip, pl.ds(row, size, stride=rows), :] = value[:, strip_of(strip)]

            unpack(totals, me)
            spans = [(across * half, half), (3 * (1 - across) * quarter, quarter), ((2 - across) * quarter, quarter)]
            if group + 1 < groups:
                spans = [(0, chips)]
            for kind, (base, count) in enumerate(spans):
                returned(group, index, kind, count - int(kind == 0)).wait_recv()

                @pl.loop(int(kind == 0), count)
                def _(step):
                    unpack(back, base + lax.rem(me + step, count))

            if there is not rest:
                for shot in range(start, start + size):
                    for strip in range(strips):
                        traces[group, shot, strip_of(strip), :] = inverse(
                            stage[strip, shot * rows : (shot + 1) * rows], tables[1]
                        )

    sent(totals, back_send_sem).wait_send()


def local(records, surface, mirror):
    chips = lax.axis_size("shot")
    cores = lax.axis_size("pair")
    groups, shots, receivers, time = records.shape
    freqs = surface.shape[0]
    parts = 2 * freqs
    tables = jnp.asarray(make_tables(freqs * chips, time))
    tall = chips * shots
    block_shape = (chips, groups, parts, shots, receivers)
    dma = pltpu.SemaphoreType.DMA
    scratch = [
        ((receivers // LANES, shots * chips * parts, LANES), jnp.float32),
        (block_shape, jnp.bfloat16),
        ((cores, groups, parts, chips, shots, receivers), jnp.bfloat16),
        ((tall, 2 * receivers), jnp.bfloat16),
        ((2 * tall, 2 * receivers), jnp.bfloat16),
        ((tall, 2 * receivers), jnp.float32),
        (block_shape, jnp.bfloat16),
        (block_shape, jnp.bfloat16),
    ]
    held_bytes = sum(math.prod(shape) * jnp.dtype(kind).itemsize for shape, kind in scratch)
    out_bytes = records.size * records.dtype.itemsize
    size = cut(shots, groups - 1, groups)[1][-1][1]
    roomy = held_bytes + 2 * out_bytes < 32 * 1024 * 1024 and size < shots
    grant = held_bytes + out_bytes + 8 * 1024 * 1024 if roomy else VMEM_BYTES
    hbm = pl.BlockSpec(memory_space=pltpu.HBM)
    vmem = pl.BlockSpec(memory_space=pltpu.VMEM)
    if roomy:
        rest_shape = (receivers // LANES, size * chips * parts, LANES)
        body = functools.partial(kernel, chips, cores)
        out_shape = [pltpu.VMEM(records.shape, jnp.bfloat16), pltpu.VMEM(rest_shape, jnp.float32)]
        out_shape.append(pltpu.VMEM(tables.shape[1:], tables.dtype))
        out_specs = [vmem] * 3
    else:
        def body(mirror_hbm, surface_hbm, tables_hbm, records_ref, out_ref, *others):
            kernel(chips, cores, mirror_hbm, surface_hbm, tables_hbm, records_ref, out_ref, None, None, *others)

        out_shape = jax.ShapeDtypeStruct(records.shape, jnp.bfloat16)
        out_specs = vmem
    result = pl.pallas_call(
        body,
        out_shape=out_shape,
        in_specs=[hbm] * 4,
        out_specs=out_specs,
        scratch_shapes=[
            *(pltpu.VMEM(shape, kind) for shape, kind in scratch),
            pltpu.VMEM(surface.shape, jnp.float32),
            pltpu.VMEM(tables.shape, tables.dtype),
            pltpu.SMEM(mirror.shape, jnp.int32),
            dma((3,)),
            dma((groups + 2,)),
            dma,
            dma,
            dma((4,)),
            dma((max(cores - 1, 1), 2)),
            dma,
            dma((groups + 5,)),
            pltpu.SemaphoreType.REGULAR,
        ],
        compiler_params=pltpu.CompilerParams(
            collective_id=0, has_side_effects=True, vmem_limit_bytes=grant
        ),
    )(
        pltpu.with_memory_space_constraint(mirror, pltpu.HBM),
        pltpu.with_memory_space_constraint(surface, pltpu.HBM),
        pltpu.with_memory_space_constraint(tables, pltpu.HBM),
        pltpu.with_memory_space_constraint(records, pltpu.HBM),
    )
    if not roomy:
        return result
    piece = (size, receivers, time)
    return pl.pallas_call(
        finish,
        out_shape=jax.ShapeDtypeStruct(records.shape, jnp.bfloat16),
        in_specs=[pl.BlockSpec(memory_space=pl.ANY), vmem, vmem],
        out_specs=hbm,
        scratch_shapes=[pltpu.VMEM(piece, jnp.bfloat16), dma((2 + max(size // 8, 1),))],
        compiler_params=pltpu.CompilerParams(
            vmem_limit_bytes=2 * math.prod(piece) + 4 * math.prod(rest_shape) + 2 * 1024 * 1024
        ),
    )(*result)


def solution(mesh):
    return jax.shard_map(
        local,
        mesh=mesh,
        in_specs=(P("pair", "shot", None, None), P("shot", None), P()),
        out_specs=P("pair", "shot", None, None),
        check_vma=False,
    )
```
